128 devices in a mesh: wide: 32 (over x, y_lo, z), narrow: 4 (over y_hi, core).
Axes of the slice: x: 4, y: 4 (y_hi: 2, y_lo: 2; y = y_hi * 2 + y_lo), z: 4, core: 2. Of those that a mesh axis runs over, the one named last changes fastest.
Arguments:
- force_columns: float32 [32, 64, 32, 16, 256], P('wide', 'narrow'), may hold values from -18 to 18
- coefficient: float32 [32, 64, 16, 256], P('wide', 'narrow'), may hold values from 0.1 to 10
- sweep_counts: int32 [32, 64], P('wide', 'narrow'), may hold values from 1 to 8, as said below
Outputs:
- self_block: float32 [32, 64, 1024], P('wide', 'narrow')
- row_block: float32 [32, 64, 1024], P('wide', 'narrow')
- column_block: float32 [32, 64, 1024], P('wide', 'narrow')
The draws below stay inside these ranges and needn't reach their ends.
Inputs may be any that keep to these rules, and one draw needn't show every extreme that they name: `sweep_counts`: A brick takes either 8 sweeps or at most 2; bricks with 8 lie only in a quarter of the brick rows (at least one row), and some brick takes 8.
All inputs are finite; a program needn't handle non-finite values.
Results may differ from the reference program's by a relative error of at most 0.0003.
Values sent between devices are 32-bit elements; how exact they have to be, the bound alone decides.
A program may use at most 256 MiB of HBM per device.

```python
import math
import jax
import jax.numpy as jnp
from jax import lax

COLUMNS = 32
EDGE_CELLS = 16
MARGIN = 4
MAX_SWEEPS = 8
BRICK_ROWS = 32
BRICK_COLS = 64


def draw_sweep_counts(key, part):
    key_light, key_rows, key_coin, key_col = jax.random.split(key, 4)
    light = jax.random.randint(key_light, (BRICK_ROWS, BRICK_COLS), 1, MAX_SWEEPS // 4 + 1)
    row_order = jax.random.permutation(key_rows, BRICK_ROWS)
    heavy_rows = row_order < max(1, BRICK_ROWS // 4)
    coin = jax.random.randint(key_coin, (BRICK_ROWS, BRICK_COLS), 0, 8) == 0
    row_pick = jnp.argmin(row_order)
    col_pick = jax.random.randint(key_col, (), 0, BRICK_COLS)
    row_index = lax.broadcasted_iota(jnp.int32, (BRICK_ROWS, BRICK_COLS), 0)
    col_index = lax.broadcasted_iota(jnp.int32, (BRICK_ROWS, BRICK_COLS), 1)
    forced = (row_index == row_pick) & (col_index == col_pick)
    heavy = heavy_rows[:, None] & (coin | forced)
    counts = jnp.where(heavy, MAX_SWEEPS, light)
    return counts.astype(jnp.int32)


def block_levels(key, dims, shards, smallest, largest):
    loudness = 1.0
    for dim, blocks in shards:
        steps = jax.random.uniform(jax.random.fold_in(jax.random.fold_in(key, 6), dim), (blocks,), jnp.float32, smallest / len(shards), largest / len(shards))
        loudness = loudness * jnp.repeat(jnp.exp(steps), dims[dim] // blocks).reshape((-1,) + (1,) * (len(dims) - 1 - dim))
    return loudness


def scatter_about(rng, dims, scale, bound, cuts=(), kind=jnp.bfloat16):
    gain = block_levels(rng, dims, cuts, -0.22, 0.18) if cuts else 1.0
    drawn = jax.random.normal(rng, dims, jnp.float32) * scale * gain
    return jnp.minimum(jnp.maximum(drawn, -bound), bound).astype(kind)


def setup_inputs(seed: int = 0) -> dict:
    arg_keys = jax.random.split(jax.random.key(seed), 4)
    force_columns = scatter_about(arg_keys[0], (BRICK_ROWS, BRICK_COLS, COLUMNS, EDGE_CELLS, EDGE_CELLS * EDGE_CELLS), 3.0, 18.0, ((0, 32), (1, 4)), jnp.float32)
    coefficient = jnp.clip(jnp.exp(math.log(10.0) - 4.6051702 * jax.random.uniform(arg_keys[1], (BRICK_ROWS, BRICK_COLS, EDGE_CELLS, EDGE_CELLS * EDGE_CELLS), jnp.float32) ** block_levels(arg_keys[1], (BRICK_ROWS, BRICK_COLS, EDGE_CELLS, EDGE_CELLS * EDGE_CELLS), ((0, 32), (1, 4)), -0.2, 0.2)), 0.1, 10.0)
    sweep_counts = draw_sweep_counts(jax.random.fold_in(arg_keys[3], 71), 0)
    return {"force_columns": force_columns, "coefficient": coefficient, "sweep_counts": sweep_counts}


REACTION = 1.0
BOUND_LOW = 0.1
BOUND_HIGH = 2.0
CENTRE = 0.5 * (BOUND_LOW + BOUND_HIGH)
HALF_WIDTH = 0.5 * (BOUND_HIGH - BOUND_LOW)
SIGMA_RATIO = CENTRE / HALF_WIDTH


def prepare(coefficient):
    edge_len = coefficient.shape[-2]
    plane_len = coefficient.shape[-1]
    x_index = lax.broadcasted_iota(jnp.int32, (edge_len, plane_len), 0)
    flat_index = lax.broadcasted_iota(jnp.int32, (edge_len, plane_len), 1)
    y_index = flat_index // edge_len
    z_index = flat_index % edge_len
    x_next = jnp.concatenate([coefficient[..., 1:, :], coefficient[..., -1:, :]], axis=-2)
    x_prev = jnp.concatenate([coefficient[..., :1, :], coefficient[..., :-1, :]], axis=-2)
    y_next = jnp.concatenate([coefficient[..., edge_len:], coefficient[..., -edge_len:]], axis=-1)
    y_prev = jnp.concatenate([coefficient[..., :edge_len], coefficient[..., :-edge_len]], axis=-1)
    z_next = jnp.where(z_index == edge_len - 1, coefficient, jnp.concatenate([coefficient[..., 1:], coefficient[..., -1:]], axis=-1))
    z_prev = jnp.where(z_index == 0, coefficient, jnp.concatenate([coefficient[..., :1], coefficient[..., :-1]], axis=-1))
    faces = ((coefficient + x_next) * 0.5, (coefficient + x_prev) * 0.5, (coefficient + y_next) * 0.5,
             (coefficient + y_prev) * 0.5, (coefficient + z_next) * 0.5, (coefficient + z_prev) * 0.5)
    diagonal = REACTION + faces[0]
    for face in faces[1:]:
        diagonal = diagonal + face
    keeps = (x_index < edge_len - 1, x_index > 0, y_index < edge_len - 1, y_index > 0, z_index < edge_len - 1, z_index > 0)
    off_terms = tuple(jnp.where(keep, face, jnp.zeros_like(face)) for keep, face in zip(keeps, faces))
    return diagonal, off_terms


def neighbours(field):
    edge_len = field.shape[-2]
    zero_row = jnp.zeros_like(field[..., :1, :])
    zero_line = jnp.zeros_like(field[..., :edge_len])
    zero_cell = jnp.zeros_like(field[..., :1])
    return (jnp.concatenate([field[..., 1:, :], zero_row], axis=-2),
            jnp.concatenate([zero_row, field[..., :-1, :]], axis=-2),
            jnp.concatenate([field[..., edge_len:], zero_line], axis=-1),
            jnp.concatenate([zero_line, field[..., :-edge_len]], axis=-1),
            jnp.concatenate([field[..., 1:], zero_cell], axis=-1),
            jnp.concatenate([zero_cell, field[..., :-1]], axis=-1))


def operate(field, diagonal, off_terms):
    result = diagonal * field
    for weight, shifted in zip(off_terms, neighbours(field)):
        result = result - weight * shifted
    return result


def start(force_block, coefficient):
    diagonal, off_terms = prepare(coefficient)
    diagonal = diagonal[:, None]
    off_terms = tuple(term[:, None] for term in off_terms)
    inverse = 1.0 / diagonal
    direction = (force_block * inverse) * (1.0 / CENTRE)
    rho_start = jnp.zeros((), jnp.float32) + 1.0 / SIGMA_RATIO
    return (jnp.zeros_like(force_block), force_block, direction, rho_start), diagonal, off_terms, inverse


def sweep_step(sweep_index, carry_state, diagonal, off_terms, inverse, counts):
    snapshot, residual, direction, rho_value = carry_state
    live = (sweep_index < counts)[:, None, None, None]
    moved = snapshot + direction
    reduced = residual - operate(direction, diagonal, off_terms)
    rho_next = 1.0 / (2.0 * SIGMA_RATIO - rho_value)
    turned = (rho_next * rho_value) * direction + (2.0 * rho_next / HALF_WIDTH) * (reduced * inverse)
    return (jnp.where(live, moved, snapshot), jnp.where(live, reduced, residual), jnp.where(live, turned, direction), rho_next)


def ramp(position, edge_len):
    return jnp.minimum(1.0, jnp.minimum((position + 0.5) / MARGIN, (edge_len - position - 0.5) / MARGIN))


def partition(edge_len):
    x_index = lax.broadcasted_iota(jnp.int32, (edge_len, edge_len * edge_len), 0)
    flat_index = lax.broadcasted_iota(jnp.int32, (edge_len, edge_len * edge_len), 1)
    x_float = x_index.astype(jnp.float32)
    y_float = (flat_index // edge_len).astype(jnp.float32)
    return ramp(x_float, edge_len) * ramp(y_float, edge_len)


def reference(force_columns, coefficient, sweep_counts):
    edge_len = EDGE_CELLS
    blend_weights = partition(edge_len)
    scale_pair = (MARGIN * edge_len * edge_len) ** -0.5

    def one_row(inputs):
        force_row, coef_row, counts = inputs
        carry_state, diagonal, off_terms, inverse = start(force_row, coef_row)
        for sweep_index in range(MAX_SWEEPS):
            carry_state = sweep_step(jnp.int32(sweep_index), carry_state, diagonal, off_terms, inverse, counts)
        weighted = carry_state[0] * blend_weights
        flattened = weighted.reshape(weighted.shape[0], COLUMNS, -1)
        self_part = jnp.einsum('bkc,blc->bkl', flattened, flattened, precision=lax.Precision.HIGHEST) / float(edge_len ** 3)
        cubed = weighted.reshape(weighted.shape[0], COLUMNS, edge_len, edge_len, edge_len)
        return (self_part.reshape(self_part.shape[0], -1), weighted[:, :, :MARGIN, :], weighted[:, :, edge_len - MARGIN:, :],
                cubed[:, :, :, :MARGIN, :], cubed[:, :, :, edge_len - MARGIN:, :])

    self_part, upper_slab, lower_slab, front_slab, back_slab = lax.map(one_row, (force_columns, coefficient, sweep_counts))
    below = jnp.roll(upper_slab, -1, axis=0)
    row_block = jnp.einsum('rbkaj,rblaj->rbkl', lower_slab, below, precision=lax.Precision.HIGHEST) * scale_pair
    beside = jnp.roll(front_slab, -1, axis=1)
    column_block = jnp.einsum('rbkxyz,rblxyz->rbkl', back_slab, beside, precision=lax.Precision.HIGHEST) * scale_pair
    return (self_part, row_block.reshape(BRICK_ROWS, BRICK_COLS, -1), column_block.reshape(BRICK_ROWS, BRICK_COLS, -1))
```

```python
import functools

import numpy as np
import jax
import jax.numpy as jnp
from jax import lax
from jax.experimental import pallas as pl
from jax.experimental.pallas import tpu as pltpu
from jax.sharding import PartitionSpec as P

MARGIN = 4
MAX_SWEEPS = 8

REACTION = 1.0
BOUND_LOW = 0.1
BOUND_HIGH = 2.0
CENTRE = 0.5 * (BOUND_LOW + BOUND_HIGH)
HALF_WIDTH = 0.5 * (BOUND_HIGH - BOUND_LOW)
SIGMA_RATIO = CENTRE / HALF_WIDTH

HIGHEST = lax.Precision.HIGHEST


def sweep_constants():
    rho = np.float32(1.0 / SIGMA_RATIO)
    two_sigma = np.float32(2.0 * SIGMA_RATIO)
    pairs = []
    for _ in range(MAX_SWEEPS):
        rho_next = np.float32(np.float32(1.0) / np.float32(two_sigma - rho))
        keep = np.float32(rho_next * rho)
        push = np.float32(np.float32(np.float32(2.0) * rho_next) / np.float32(HALF_WIDTH))
        pairs.append((float(keep), float(push)))
        rho = rho_next
    return pairs


def from_behind(block, axis, distance):
    devices = range(lax.axis_size(axis))
    route = [((i - distance) % len(devices), i) for i in devices]
    return lax.ppermute(block, axis, route)


def prepare(coefficient):
    edge_len = coefficient.shape[-2]
    plane_len = coefficient.shape[-1]
    x_index = lax.broadcasted_iota(jnp.int32, (edge_len, plane_len), 0)
    flat_index = lax.broadcasted_iota(jnp.int32, (edge_len, plane_len), 1)
    y_index = flat_index // edge_len
    z_index = flat_index % edge_len
    x_next = jnp.concatenate([coefficient[..., 1:, :], coefficient[..., -1:, :]], axis=-2)
    x_prev = jnp.concatenate([coefficient[..., :1, :], coefficient[..., :-1, :]], axis=-2)
    y_next = jnp.concatenate([coefficient[..., edge_len:], coefficient[..., -edge_len:]], axis=-1)
    y_prev = jnp.concatenate([coefficient[..., :edge_len], coefficient[..., :-edge_len]], axis=-1)
    z_next = jnp.where(
        z_index == edge_len - 1,
        coefficient,
        jnp.concatenate([coefficient[..., 1:], coefficient[..., -1:]], axis=-1),
    )
    z_prev = jnp.where(
        z_index == 0,
        coefficient,
        jnp.concatenate([coefficient[..., :1], coefficient[..., :-1]], axis=-1),
    )
    faces = (
        (coefficient + x_next) * 0.5,
        (coefficient + x_prev) * 0.5,
        (coefficient + y_next) * 0.5,
        (coefficient + y_prev) * 0.5,
        (coefficient + z_next) * 0.5,
        (coefficient + z_prev) * 0.5,
    )
    diagonal = REACTION + faces[0]
    for face in faces[1:]:
        diagonal = diagonal + face
    keeps = (
        x_index < edge_len - 1,
        x_index > 0,
        y_index < edge_len - 1,
        y_index > 0,
        z_index < edge_len - 1,
        z_index > 0,
    )
    off_terms = tuple(
        (jnp.where(keep, face, jnp.zeros_like(face)) for keep, face in zip(keeps, faces))
    )
    return (diagonal, off_terms)


def ramp(position, edge_len):
    return jnp.minimum(
        1.0, jnp.minimum((position + 0.5) / MARGIN, (edge_len - position - 0.5) / MARGIN)
    )


def partition(edge_len):
    x_index = lax.broadcasted_iota(jnp.int32, (edge_len, edge_len * edge_len), 0)
    flat_index = lax.broadcasted_iota(jnp.int32, (edge_len, edge_len * edge_len), 1)
    x_float = x_index.astype(jnp.float32)
    y_float = (flat_index // edge_len).astype(jnp.float32)
    return ramp(x_float, edge_len) * ramp(y_float, edge_len)


def gram(a, b):
    return lax.dot_general(
        a, b, (((1,), (1,)), ((), ())), precision=HIGHEST, preferred_element_type=jnp.float32
    )


def brick_kernel(
    counts_ref, force_lo, force_hi, terms_ref, blend_ref,
    self_ref, up_ref, lo_ref, col_ref, front_ref, back_ref,
    snap, resid, direc, terms, behind,
    *, edge_len, columns,
):
    b = pl.program_id(0)
    last = pl.num_programs(0) - 1
    count = counts_ref[b]
    groups = columns // 8
    plane = edge_len * edge_len
    scale_pair = float((MARGIN * edge_len * edge_len) ** (-0.5))

    def rep(row):
        return jnp.concatenate([row] * groups, axis=0)

    for k in range(8):
        for x in range(edge_len):
            terms[k, x] = jnp.broadcast_to(terms_ref[k, x : x + 1, :], (8, plane))

    start_scale = float(np.float32(1.0 / CENTRE))
    for x in range(edge_len):
        rows = pl.ds(x, columns, stride=edge_len)
        f = jnp.concatenate([force_lo[rows, :], force_hi[rows, :]], axis=1)
        resid[x] = f
        direc[0, x] = f * rep(terms[7, x]) * start_scale
        snap[x] = jnp.zeros_like(f)

    for t, (keep, push) in enumerate(sweep_constants()):
        src, dst = t % 2, (t + 1) % 2

        @pl.when(t < count)
        def _():
            def one_plane(x, carry):
                xm = jnp.maximum(x - 1, 0)
                xp = jnp.minimum(x + 1, edge_len - 1)
                d0 = direc[src, x]
                res = rep(terms[0, x]) * d0
                res = res - rep(terms[1, x]) * direc[src, xp]
                res = res - rep(terms[2, x]) * direc[src, xm]
                res = res - rep(terms[3, x]) * pltpu.roll(d0, plane - edge_len, 1)
                res = res - rep(terms[4, x]) * pltpu.roll(d0, edge_len, 1)
                res = res - rep(terms[5, x]) * pltpu.roll(d0, plane - 1, 1)
                res = res - rep(terms[6, x]) * pltpu.roll(d0, 1, 1)
                r = resid[x] - res
                resid[x] = r
                snap[x] = snap[x] + d0
                direc[dst, x] = keep * d0 + push * (r * rep(terms[7, x]))
                return carry

            lax.fori_loop(0, edge_len, one_plane, 0)

    lane = lax.broadcasted_iota(jnp.int32, (columns, plane), 1)
    front_lanes = lane < MARGIN * edge_len

    def finish(x, acc):
        g, c = acc
        w = snap[x] * jnp.broadcast_to(blend_ref[pl.ds(x, 1), :], (columns, plane))
        snap[x] = w
        g = g + gram(w, w)
        front = jnp.where(front_lanes, w, 0.0)
        c = c + gram(behind[x], front)
        behind[x] = jnp.where(front_lanes, pltpu.roll(w, MARGIN * edge_len, 1), 0.0)
        return g, c

    zero = jnp.zeros((columns, columns), jnp.float32)
    g, c = lax.fori_loop(0, edge_len, finish, (zero, zero))
    self_ref[...] = g / float(edge_len**3)

    @pl.when(b > 0)
    def _():
        col_ref[b - 1] = c * scale_pair

    for a in range(MARGIN):
        up_ref[a] = snap[a]
        lo_ref[a] = snap[edge_len - MARGIN + a]

    @pl.when(b == 0)
    def _():
        for x in range(edge_len):
            front_ref[x] = jnp.where(front_lanes, snap[x], 0.0)

    @pl.when(b == last)
    def _():
        for x in range(edge_len):
            back_ref[x] = behind[x]


def run_bricks(force, coefficient, counts):
    bricks, columns, edge_len, plane = force.shape
    diagonal, off_terms = prepare(coefficient)
    inverse = 1.0 / diagonal
    terms_in = jnp.stack((diagonal,) + off_terms + (inverse,), axis=1)
    blend = partition(edge_len)
    force2 = force.reshape(bricks, columns * edge_len, plane)
    kernel = functools.partial(brick_kernel, edge_len=edge_len, columns=columns)
    f32 = jnp.float32
    out_shape = (
        jax.ShapeDtypeStruct((bricks, columns, columns), f32),
        jax.ShapeDtypeStruct((bricks, MARGIN, columns, plane), f32),
        jax.ShapeDtypeStruct((bricks, MARGIN, columns, plane), f32),
        jax.ShapeDtypeStruct((bricks, columns, columns), f32),
        jax.ShapeDtypeStruct((edge_len, columns, plane), f32),
        jax.ShapeDtypeStruct((edge_len, columns, plane), f32),
    )
    grid_spec = pltpu.PrefetchScalarGridSpec(
        num_scalar_prefetch=1,
        grid=(bricks,),
        in_specs=[
            pl.BlockSpec((None, columns * edge_len, 128), lambda b, c: (b, 0, 0)),
            pl.BlockSpec((None, columns * edge_len, 128), lambda b, c: (b, 0, 1)),
            pl.BlockSpec((None, 8, edge_len, plane), lambda b, c: (b, 0, 0, 0)),
            pl.BlockSpec((edge_len, plane), lambda b, c: (0, 0)),
        ],
        out_specs=[
            pl.BlockSpec((None, columns, columns), lambda b, c: (b, 0, 0)),
            pl.BlockSpec((None, MARGIN, columns, plane), lambda b, c: (b, 0, 0, 0)),
            pl.BlockSpec((None, MARGIN, columns, plane), lambda b, c: (b, 0, 0, 0)),
            pl.BlockSpec((bricks, columns, columns), lambda b, c: (0, 0, 0)),
            pl.BlockSpec((edge_len, columns, plane), lambda b, c: (0, 0, 0)),
            pl.BlockSpec((edge_len, columns, plane), lambda b, c: (0, 0, 0)),
        ],
        scratch_shapes=[
            pltpu.VMEM((edge_len, columns, plane), f32),
            pltpu.VMEM((edge_len, columns, plane), f32),
            pltpu.VMEM((2, edge_len, columns, plane), f32),
            pltpu.VMEM((8, edge_len, 8, plane), f32),
            pltpu.VMEM((edge_len, columns, plane), f32),
        ],
    )
    return pl.pallas_call(
        kernel,
        grid_spec=grid_spec,
        out_shape=out_shape,
        compiler_params=pltpu.CompilerParams(dimension_semantics=("arbitrary",)),
    )(counts, force2, force2, terms_in, blend)


def on_device(force_columns, coefficient, sweep_counts):
    bricks = force_columns.shape[1]
    columns = force_columns.shape[2]
    edge_len = force_columns.shape[3]
    scale_pair = (MARGIN * edge_len * edge_len) ** (-0.5)
    self_part, upper, lower, col_part, front, back = run_bricks(
        force_columns[0], coefficient[0], sweep_counts[0]
    )
    below = from_behind(upper, "wide", -1)
    row_part = (
        jnp.einsum("bakc,balc->bkl", lower, below, precision=HIGHEST) * scale_pair
    )
    arrived = from_behind(front, "narrow", -1)
    last_col = jnp.einsum("xkc,xlc->kl", back, arrived, precision=HIGHEST) * scale_pair
    col_part = jnp.concatenate([col_part[:-1], last_col[None]], axis=0)
    return (
        self_part.reshape(1, bricks, -1),
        row_part.reshape(1, bricks, -1),
        col_part.reshape(1, bricks, -1),
    )


def solution(mesh):
    in_specs = (
        P("wide", "narrow", None, None, None),
        P("wide", "narrow", None, None),
        P("wide", "narrow"),
    )
    out_specs = (P("wide", "narrow", None), P("wide", "narrow", None), P("wide", "narrow", None))
    return jax.shard_map(
        on_device, mesh=mesh, in_specs=in_specs, out_specs=out_specs, check_vma=False
    )
```

```python
import functools

import numpy as np
import jax
import jax.numpy as jnp
from jax import lax
from jax.experimental import pallas as pl
from jax.experimental.pallas import tpu as pltpu
from jax.sharding import PartitionSpec as P

MARGIN = 4
MAX_SWEEPS = 8

REACTION = 1.0
BOUND_LOW = 0.1
BOUND_HIGH = 2.0
CENTRE = 0.5 * (BOUND_LOW + BOUND_HIGH)
HALF_WIDTH = 0.5 * (BOUND_HIGH - BOUND_LOW)
SIGMA_RATIO = CENTRE / HALF_WIDTH

HIGHEST = lax.Precision.HIGHEST


def sweep_constants():
    rho = np.float32(1.0 / SIGMA_RATIO)
    two_sigma = np.float32(2.0 * SIGMA_RATIO)
    pairs = []
    for _ in range(MAX_SWEEPS):
        rho_next = np.float32(np.float32(1.0) / np.float32(two_sigma - rho))
        keep = np.float32(rho_next * rho)
        push = np.float32(np.float32(np.float32(2.0) * rho_next) / np.float32(HALF_WIDTH))
        pairs.append((float(keep), float(push)))
        rho = rho_next
    return pairs


def from_behind(block, axis, distance):
    devices = range(lax.axis_size(axis))
    route = [((i - distance) % len(devices), i) for i in devices]
    return lax.ppermute(block, axis, route)


def prepare(coefficient):
    edge_len = coefficient.shape[-2]
    plane_len = coefficient.shape[-1]
    x_index = lax.broadcasted_iota(jnp.int32, (edge_len, plane_len), 0)
    flat_index = lax.broadcasted_iota(jnp.int32, (edge_len, plane_len), 1)
    y_index = flat_index // edge_len
    z_index = flat_index % edge_len
    x_next = jnp.concatenate([coefficient[..., 1:, :], coefficient[..., -1:, :]], axis=-2)
    x_prev = jnp.concatenate([coefficient[..., :1, :], coefficient[..., :-1, :]], axis=-2)
    y_next = jnp.concatenate([coefficient[..., edge_len:], coefficient[..., -edge_len:]], axis=-1)
    y_prev = jnp.concatenate([coefficient[..., :edge_len], coefficient[..., :-edge_len]], axis=-1)
    z_next = jnp.where(
        z_index == edge_len - 1,
        coefficient,
        jnp.concatenate([coefficient[..., 1:], coefficient[..., -1:]], axis=-1),
    )
    z_prev = jnp.where(
        z_index == 0,
        coefficient,
        jnp.concatenate([coefficient[..., :1], coefficient[..., :-1]], axis=-1),
    )
    faces = (
        (coefficient + x_next) * 0.5,
        (coefficient + x_prev) * 0.5,
        (coefficient + y_next) * 0.5,
        (coefficient + y_prev) * 0.5,
        (coefficient + z_next) * 0.5,
        (coefficient + z_prev) * 0.5,
    )
    diagonal = REACTION + faces[0]
    for face in faces[1:]:
        diagonal = diagonal + face
    keeps = (
        x_index < edge_len - 1,
        x_index > 0,
        y_index < edge_len - 1,
        y_index > 0,
        z_index < edge_len - 1,
        z_index > 0,
    )
    off_terms = tuple(
        (jnp.where(keep, face, jnp.zeros_like(face)) for keep, face in zip(keeps, faces))
    )
    return (diagonal, off_terms)


def ramp(position, edge_len):
    return jnp.minimum(
        1.0, jnp.minimum((position + 0.5) / MARGIN, (edge_len - position - 0.5) / MARGIN)
    )


def partition(edge_len):
    x_index = lax.broadcasted_iota(jnp.int32, (edge_len, edge_len * edge_len), 0)
    flat_index = lax.broadcasted_iota(jnp.int32, (edge_len, edge_len * edge_len), 1)
    x_float = x_index.astype(jnp.float32)
    y_float = (flat_index // edge_len).astype(jnp.float32)
    return ramp(x_float, edge_len) * ramp(y_float, edge_len)


def gram(a, b):
    return lax.dot_general(
        a, b, (((1,), (1,)), ((), ())), precision=HIGHEST, preferred_element_type=jnp.float32
    )


def brick_kernel(
    counts_ref, consts_ref, force_lo, force_hi, terms_ref, blend_ref,
    self_ref, up_ref, lo_ref, col_ref, front_ref, back_ref,
    snap, resid, direc, terms, behind,
    *, edge_len, columns,
):
    b = pl.program_id(0)
    last = pl.num_programs(0) - 1
    count = jnp.minimum(counts_ref[b], MAX_SWEEPS)
    groups = columns // 8
    plane = edge_len * edge_len
    band = MARGIN * edge_len
    scale_pair = float((MARGIN * edge_len * edge_len) ** (-0.5))

    def rep(row):
        return jnp.concatenate([row] * groups, axis=0)

    for k in range(8):
        for x in range(edge_len):
            terms[k, x] = jnp.broadcast_to(terms_ref[k, x : x + 1, :], (8, plane))

    start_scale = float(np.float32(1.0 / CENTRE))
    for x in range(edge_len):
        rows = pl.ds(x, columns, stride=edge_len)
        f = jnp.concatenate([force_lo[rows, :], force_hi[rows, :]], axis=1)
        resid[x] = f
        direc[x] = f * rep(terms[7, x]) * start_scale
        snap[x] = jnp.zeros_like(f)

    def sweep(t, carry):
        keep = consts_ref[0, t]
        push = consts_ref[1, t]
        prev = None
        cur = direc[0]
        for x in range(edge_len):
            nxt = direc[x + 1] if x + 1 < edge_len else None
            res = rep(terms[0, x]) * cur
            if nxt is not None:
                res = res - rep(terms[1, x]) * nxt
            if prev is not None:
                res = res - rep(terms[2, x]) * prev
            res = res - rep(terms[3, x]) * pltpu.roll(cur, plane - edge_len, 1)
            res = res - rep(terms[4, x]) * pltpu.roll(cur, edge_len, 1)
            res = res - rep(terms[5, x]) * pltpu.roll(cur, plane - 1, 1)
            res = res - rep(terms[6, x]) * pltpu.roll(cur, 1, 1)
            r = resid[x] - res
            resid[x] = r
            snap[x] = snap[x] + cur
            direc[x] = keep * cur + push * (r * rep(terms[7, x]))
            prev, cur = cur, nxt
        return carry

    lax.fori_loop(0, count, sweep, 0)

    lane = lax.broadcasted_iota(jnp.int32, (columns, plane), 1)
    quarter = [(lane >= band * j) & (lane < band * (j + 1)) for j in range(4)]
    weighted = []
    for x in range(edge_len):
        w = snap[x] * jnp.broadcast_to(blend_ref[x : x + 1, :], (columns, plane))
        weighted.append(w)
    fronts, backs = [], []
    for i in range(edge_len // 4):
        ws = weighted[4 * i : 4 * i + 4]
        f = jnp.where(quarter[0], ws[0], 0.0)
        k = jnp.where(quarter[3], ws[3], 0.0)
        for j in range(1, 4):
            f = jnp.where(quarter[j], pltpu.roll(ws[j], band * j, 1), f)
        for j in range(3):
            k = jnp.where(quarter[j], pltpu.roll(ws[j], band * (j + 1), 1), k)
        fronts.append(f)
        backs.append(k)
    front = jnp.concatenate(fronts, axis=1)
    back = jnp.concatenate(backs, axis=1)
    whole = jnp.concatenate(weighted, axis=1)
    self_ref[...] = gram(whole, whole) / float(edge_len**3)
    up_ref[...] = jnp.concatenate(weighted[:MARGIN], axis=1)
    lo_ref[...] = jnp.concatenate(weighted[edge_len - MARGIN :], axis=1)

    @pl.when(b > 0)
    def _():
        col_ref[b - 1] = gram(behind[...], front) * scale_pair

    behind[...] = back

    @pl.when(b == 0)
    def _():
        front_ref[...] = front

    @pl.when(b == last)
    def _():
        back_ref[...] = back


def run_bricks(force, coefficient, counts):
    bricks, columns, edge_len, plane = force.shape
    diagonal, off_terms = prepare(coefficient)
    inverse = 1.0 / diagonal
    terms_in = jnp.stack((diagonal,) + off_terms + (inverse,), axis=1)
    blend = partition(edge_len)
    consts = jnp.asarray(np.array(sweep_constants(), np.float32).T)
    force2 = force.reshape(bricks, columns * edge_len, plane)
    kernel = functools.partial(brick_kernel, edge_len=edge_len, columns=columns)
    f32 = jnp.float32
    slab = MARGIN * plane
    band = plane * (edge_len // 4)
    out_shape = (
        jax.ShapeDtypeStruct((bricks, columns, columns), f32),
        jax.ShapeDtypeStruct((bricks, columns, slab), f32),
        jax.ShapeDtypeStruct((bricks, columns, slab), f32),
        jax.ShapeDtypeStruct((bricks, columns, columns), f32),
        jax.ShapeDtypeStruct((columns, band), f32),
        jax.ShapeDtypeStruct((columns, band), f32),
    )
    grid_spec = pltpu.PrefetchScalarGridSpec(
        num_scalar_prefetch=1,
        grid=(bricks,),
        in_specs=[
            pl.BlockSpec(memory_space=pltpu.SMEM),
            pl.BlockSpec((None, columns * edge_len, 128), lambda b, c: (b, 0, 0)),
            pl.BlockSpec((None, columns * edge_len, 128), lambda b, c: (b, 0, 1)),
            pl.BlockSpec((None, 8, edge_len, plane), lambda b, c: (b, 0, 0, 0)),
            pl.BlockSpec((edge_len, plane), lambda b, c: (0, 0)),
        ],
        out_specs=[
            pl.BlockSpec((None, columns, columns), lambda b, c: (b, 0, 0)),
            pl.BlockSpec((None, columns, slab), lambda b, c: (b, 0, 0)),
            pl.BlockSpec((None, columns, slab), lambda b, c: (b, 0, 0)),
            pl.BlockSpec((bricks, columns, columns), lambda b, c: (0, 0, 0)),
            pl.BlockSpec((columns, band), lambda b, c: (0, 0)),
            pl.BlockSpec((columns, band), lambda b, c: (0, 0)),
        ],
        scratch_shapes=[
            pltpu.VMEM((edge_len, columns, plane), f32),
            pltpu.VMEM((edge_len, columns, plane), f32),
            pltpu.VMEM((edge_len, columns, plane), f32),
            pltpu.VMEM((8, edge_len, 8, plane), f32),
            pltpu.VMEM((columns, band), f32),
        ],
    )
    return pl.pallas_call(
        kernel,
        grid_spec=grid_spec,
        out_shape=out_shape,
        compiler_params=pltpu.CompilerParams(dimension_semantics=("arbitrary",)),
    )(counts, consts, force2, force2, terms_in, blend)


def on_device(force_columns, coefficient, sweep_counts):
    bricks = force_columns.shape[1]
    columns = force_columns.shape[2]
    edge_len = force_columns.shape[3]
    scale_pair = (MARGIN * edge_len * edge_len) ** (-0.5)
    self_part, upper, lower, col_part, front, back = run_bricks(
        force_columns[0], coefficient[0], sweep_counts[0]
    )
    below = from_behind(upper, "wide", -1)
    row_part = jnp.einsum("bkc,blc->bkl", lower, below, precision=HIGHEST) * scale_pair
    arrived = from_behind(front, "narrow", -1)
    last_col = gram(back, arrived) * scale_pair
    col_part = jnp.concatenate([col_part[:-1], last_col[None]], axis=0)
    return (
        self_part.reshape(1, bricks, -1),
        row_part.reshape(1, bricks, -1),
        col_part.reshape(1, bricks, -1),
    )


def solution(mesh):
    in_specs = (
        P("wide", "narrow", None, None, None),
        P("wide", "narrow", None, None),
        P("wide", "narrow"),
    )
    out_specs = (P("wide", "narrow", None), P("wide", "narrow", None), P("wide", "narrow", None))
    return jax.shard_map(
        on_device, mesh=mesh, in_specs=in_specs, out_specs=out_specs, check_vma=False
    )
```

```python
import functools

import numpy as np
import jax
import jax.numpy as jnp
from jax import lax
from jax.experimental import pallas as pl
from jax.experimental.pallas import tpu as pltpu
from jax.sharding import PartitionSpec as P

MARGIN = 4
MAX_SWEEPS = 8

REACTION = 1.0
BOUND_LOW = 0.1
BOUND_HIGH = 2.0
CENTRE = 0.5 * (BOUND_LOW + BOUND_HIGH)
HALF_WIDTH = 0.5 * (BOUND_HIGH - BOUND_LOW)
SIGMA_RATIO = CENTRE / HALF_WIDTH

HIGHEST = lax.Precision.HIGHEST


def sweep_constants():
    rho = np.float32(1.0 / SIGMA_RATIO)
    two_sigma = np.float32(2.0 * SIGMA_RATIO)
    pairs = []
    for _ in range(MAX_SWEEPS):
        rho_next = np.float32(np.float32(1.0) / np.float32(two_sigma - rho))
        keep = np.float32(rho_next * rho)
        push = np.float32(np.float32(np.float32(2.0) * rho_next) / np.float32(HALF_WIDTH))
        pairs.append((float(keep), float(push)))
        rho = rho_next
    return pairs


def from_behind(block, axis, distance):
    devices = range(lax.axis_size(axis))
    route = [((i - distance) % len(devices), i) for i in devices]
    return lax.ppermute(block, axis, route)


def prepare(coefficient):
    edge_len = coefficient.shape[-2]
    plane_len = coefficient.shape[-1]
    x_index = lax.broadcasted_iota(jnp.int32, (edge_len, plane_len), 0)
    flat_index = lax.broadcasted_iota(jnp.int32, (edge_len, plane_len), 1)
    y_index = flat_index // edge_len
    z_index = flat_index % edge_len
    x_next = jnp.concatenate([coefficient[..., 1:, :], coefficient[..., -1:, :]], axis=-2)
    x_prev = jnp.concatenate([coefficient[..., :1, :], coefficient[..., :-1, :]], axis=-2)
    y_next = jnp.concatenate([coefficient[..., edge_len:], coefficient[..., -edge_len:]], axis=-1)
    y_prev = jnp.concatenate([coefficient[..., :edge_len], coefficient[..., :-edge_len]], axis=-1)
    z_next = jnp.where(
        z_index == edge_len - 1,
        coefficient,
        jnp.concatenate([coefficient[..., 1:], coefficient[..., -1:]], axis=-1),
    )
    z_prev = jnp.where(
        z_index == 0,
        coefficient,
        jnp.concatenate([coefficient[..., :1], coefficient[..., :-1]], axis=-1),
    )
    faces = (
        (coefficient + x_next) * 0.5,
        (coefficient + x_prev) * 0.5,
        (coefficient + y_next) * 0.5,
        (coefficient + y_prev) * 0.5,
        (coefficient + z_next) * 0.5,
        (coefficient + z_prev) * 0.5,
    )
    diagonal = REACTION + faces[0]
    for face in faces[1:]:
        diagonal = diagonal + face
    keeps = (
        x_index < edge_len - 1,
        x_index > 0,
        y_index < edge_len - 1,
        y_index > 0,
        z_index < edge_len - 1,
        z_index > 0,
    )
    off_terms = tuple(
        (jnp.where(keep, face, jnp.zeros_like(face)) for keep, face in zip(keeps, faces))
    )
    return (diagonal, off_terms)


def ramp(position, edge_len):
    return jnp.minimum(
        1.0, jnp.minimum((position + 0.5) / MARGIN, (edge_len - position - 0.5) / MARGIN)
    )


def partition(edge_len):
    x_index = lax.broadcasted_iota(jnp.int32, (edge_len, edge_len * edge_len), 0)
    flat_index = lax.broadcasted_iota(jnp.int32, (edge_len, edge_len * edge_len), 1)
    x_float = x_index.astype(jnp.float32)
    y_float = (flat_index // edge_len).astype(jnp.float32)
    return ramp(x_float, edge_len) * ramp(y_float, edge_len)


def gram(a, b):
    return lax.dot_general(
        a, b, (((1,), (1,)), ((), ())), precision=HIGHEST, preferred_element_type=jnp.float32
    )


def brick_kernel(
    counts_ref, consts_ref, force_lo, force_hi, terms_ref, blend_ref,
    self_ref, up_ref, lo_ref, col_ref, front_ref, back_ref,
    snap, resid, direc, terms, behind,
    *, edge_len, columns, first,
):
    b = pl.program_id(0)
    last = pl.num_programs(0) - 1
    count = jnp.minimum(counts_ref[first + b], MAX_SWEEPS)
    groups = columns // 8
    plane = edge_len * edge_len
    band = MARGIN * edge_len
    scale_pair = float((MARGIN * edge_len * edge_len) ** (-0.5))

    def rep(row):
        return jnp.concatenate([row] * groups, axis=0)

    for k in range(8):
        for x in range(edge_len):
            terms[k, x] = jnp.broadcast_to(terms_ref[k, x : x + 1, :], (8, plane))

    start_scale = float(np.float32(1.0 / CENTRE))
    for x in range(edge_len):
        rows = pl.ds(x, columns, stride=edge_len)
        f = jnp.concatenate([force_lo[rows, :], force_hi[rows, :]], axis=1)
        resid[x] = f
        direc[x] = f * rep(terms[7, x]) * start_scale
        snap[x] = jnp.zeros_like(f)

    def sweep(t, carry):
        keep = consts_ref[0, t]
        push = consts_ref[1, t]
        prev = None
        cur = direc[0]
        for x in range(edge_len):
            nxt = direc[x + 1] if x + 1 < edge_len else None
            res = rep(terms[0, x]) * cur
            if nxt is not None:
                res = res - rep(terms[1, x]) * nxt
            if prev is not None:
                res = res - rep(terms[2, x]) * prev
            res = res - rep(terms[3, x]) * pltpu.roll(cur, plane - edge_len, 1)
            res = res - rep(terms[4, x]) * pltpu.roll(cur, edge_len, 1)
            res = res - rep(terms[5, x]) * pltpu.roll(cur, plane - 1, 1)
            res = res - rep(terms[6, x]) * pltpu.roll(cur, 1, 1)
            r = resid[x] - res
            resid[x] = r
            snap[x] = snap[x] + cur
            direc[x] = keep * cur + push * (r * rep(terms[7, x]))
            prev, cur = cur, nxt
        return carry

    lax.fori_loop(0, count, sweep, 0)

    lane = lax.broadcasted_iota(jnp.int32, (columns, plane), 1)
    quarter = [(lane >= band * j) & (lane < band * (j + 1)) for j in range(4)]
    weighted = []
    for x in range(edge_len):
        w = snap[x] * jnp.broadcast_to(blend_ref[x : x + 1, :], (columns, plane))
        weighted.append(w)
    fronts, backs = [], []
    for i in range(edge_len // 4):
        ws = weighted[4 * i : 4 * i + 4]
        f = jnp.where(quarter[0], ws[0], 0.0)
        k = jnp.where(quarter[3], ws[3], 0.0)
        for j in range(1, 4):
            f = jnp.where(quarter[j], pltpu.roll(ws[j], band * j, 1), f)
        for j in range(3):
            k = jnp.where(quarter[j], pltpu.roll(ws[j], band * (j + 1), 1), k)
        fronts.append(f)
        backs.append(k)
    front = jnp.concatenate(fronts, axis=1)
    back = jnp.concatenate(backs, axis=1)
    whole = jnp.concatenate(weighted, axis=1)
    self_ref[...] = gram(whole, whole) / float(edge_len**3)
    up_ref[...] = jnp.concatenate(weighted[:MARGIN], axis=1)
    lo_ref[...] = jnp.concatenate(weighted[edge_len - MARGIN :], axis=1)

    @pl.when(b > 0)
    def _():
        col_ref[b - 1] = gram(behind[...], front) * scale_pair

    behind[...] = back

    @pl.when(b == 0)
    def _():
        front_ref[...] = front

    @pl.when(b == last)
    def _():
        back_ref[...] = back


def run_chunk(force2, terms_in, blend, consts, counts, first, size):
    bricks, rows2, _ = force2.shape
    edge_len, plane = blend.shape
    columns = rows2 // edge_len
    kernel = functools.partial(brick_kernel, edge_len=edge_len, columns=columns, first=first)
    f32 = jnp.float32
    slab = MARGIN * plane
    band = plane * (edge_len // 4)
    out_shape = (
        jax.ShapeDtypeStruct((size, columns, columns), f32),
        jax.ShapeDtypeStruct((size, columns, slab), f32),
        jax.ShapeDtypeStruct((size, columns, slab), f32),
        jax.ShapeDtypeStruct((size, columns, columns), f32),
        jax.ShapeDtypeStruct((columns, band), f32),
        jax.ShapeDtypeStruct((columns, band), f32),
    )
    grid_spec = pltpu.PrefetchScalarGridSpec(
        num_scalar_prefetch=1,
        grid=(size,),
        in_specs=[
            pl.BlockSpec(memory_space=pltpu.SMEM),
            pl.BlockSpec((None, rows2, 128), lambda b, c: (first + b, 0, 0)),
            pl.BlockSpec((None, rows2, 128), lambda b, c: (first + b, 0, 1)),
            pl.BlockSpec((None, 8, edge_len, plane), lambda b, c: (first + b, 0, 0, 0)),
            pl.BlockSpec((edge_len, plane), lambda b, c: (0, 0)),
        ],
        out_specs=[
            pl.BlockSpec((None, columns, columns), lambda b, c: (b, 0, 0)),
            pl.BlockSpec((None, columns, slab), lambda b, c: (b, 0, 0)),
            pl.BlockSpec((None, columns, slab), lambda b, c: (b, 0, 0)),
            pl.BlockSpec((size, columns, columns), lambda b, c: (0, 0, 0)),
            pl.BlockSpec((columns, band), lambda b, c: (0, 0)),
            pl.BlockSpec((columns, band), lambda b, c: (0, 0)),
        ],
        scratch_shapes=[
            pltpu.VMEM((edge_len, columns, plane), f32),
            pltpu.VMEM((edge_len, columns, plane), f32),
            pltpu.VMEM((edge_len, columns, plane), f32),
            pltpu.VMEM((8, edge_len, 8, plane), f32),
            pltpu.VMEM((columns, band), f32),
        ],
    )
    flops = size * (columns * plane * edge_len * 40 + 2 * columns * columns * plane * edge_len * 6)
    return pl.pallas_call(
        kernel,
        grid_spec=grid_spec,
        out_shape=out_shape,
        compiler_params=pltpu.CompilerParams(dimension_semantics=("arbitrary",)),
        cost_estimate=pl.CostEstimate(
            flops=flops, transcendentals=0, bytes_accessed=size * columns * plane * edge_len * 4
        ),
    )(counts, consts, force2, force2, terms_in, blend)


CHUNK = 4


def on_device(force_columns, coefficient, sweep_counts):
    force = force_columns[0]
    bricks, columns, edge_len, plane = force.shape
    scale_pair = (MARGIN * edge_len * edge_len) ** (-0.5)
    diagonal, off_terms = prepare(coefficient[0])
    inverse = 1.0 / diagonal
    terms_in = jnp.stack((diagonal,) + off_terms + (inverse,), axis=1)
    blend = partition(edge_len)
    consts = jnp.asarray(np.array(sweep_constants(), np.float32).T)
    force2 = force.reshape(bricks, columns * edge_len, plane)
    counts = sweep_counts[0]
    size = CHUNK if bricks % CHUNK == 0 else bricks
    selfs, cols, fronts, backs, rows = [], [], [], [], []
    for first in range(0, bricks, size):
        s_c, up_c, lo_c, col_c, front_c, back_c = run_chunk(
            force2, terms_in, blend, consts, counts, first, size
        )
        up_in = from_behind(up_c, "wide", -1)
        rows.append(gram3(lo_c, up_in) * scale_pair)
        selfs.append(s_c)
        cols.append(col_c)
        fronts.append(front_c)
        backs.append(back_c)
    fronts.append(from_behind(fronts[0], "narrow", -1))
    joins = gram3(jnp.stack(backs), jnp.stack(fronts[1:])) * scale_pair
    col_parts = []
    for c in range(len(cols)):
        col_parts.append(cols[c][:-1])
        col_parts.append(joins[c][None])
    row_parts = rows
    self_part = jnp.concatenate(selfs, axis=0)
    row_part = jnp.concatenate(row_parts, axis=0)
    col_part = jnp.concatenate(col_parts, axis=0)
    return (
        self_part.reshape(1, bricks, -1),
        row_part.reshape(1, bricks, -1),
        col_part.reshape(1, bricks, -1),
    )


def gram3(a, b):
    return jnp.einsum("bkc,blc->bkl", a, b, precision=HIGHEST)


def solution(mesh):
    in_specs = (
        P("wide", "narrow", None, None, None),
        P("wide", "narrow", None, None),
        P("wide", "narrow"),
    )
    out_specs = (P("wide", "narrow", None), P("wide", "narrow", None), P("wide", "narrow", None))
    return jax.shard_map(
        on_device, mesh=mesh, in_specs=in_specs, out_specs=out_specs, check_vma=False
    )
```

```python
import functools

import numpy as np
import jax
import jax.numpy as jnp
from jax import lax
from jax.experimental import pallas as pl
from jax.experimental.pallas import tpu as pltpu
from jax.sharding import PartitionSpec as P

MARGIN = 4
MAX_SWEEPS = 8

REACTION = 1.0
BOUND_LOW = 0.1
BOUND_HIGH = 2.0
CENTRE = 0.5 * (BOUND_LOW + BOUND_HIGH)
HALF_WIDTH = 0.5 * (BOUND_HIGH - BOUND_LOW)
SIGMA_RATIO = CENTRE / HALF_WIDTH

HIGHEST = lax.Precision.HIGHEST


def sweep_constants():
    rho = np.float32(1.0 / SIGMA_RATIO)
    two_sigma = np.float32(2.0 * SIGMA_RATIO)
    pairs = []
    for _ in range(MAX_SWEEPS):
        rho_next = np.float32(np.float32(1.0) / np.float32(two_sigma - rho))
        keep = np.float32(rho_next * rho)
        push = np.float32(np.float32(np.float32(2.0) * rho_next) / np.float32(HALF_WIDTH))
        pairs.append((float(keep), float(push)))
        rho = rho_next
    return pairs


def from_behind(block, axis, distance):
    devices = range(lax.axis_size(axis))
    route = [((i - distance) % len(devices), i) for i in devices]
    return lax.ppermute(block, axis, route)


def prepare(coefficient):
    edge_len = coefficient.shape[-2]
    plane_len = coefficient.shape[-1]
    x_index = lax.broadcasted_iota(jnp.int32, (edge_len, plane_len), 0)
    flat_index = lax.broadcasted_iota(jnp.int32, (edge_len, plane_len), 1)
    y_index = flat_index // edge_len
    z_index = flat_index % edge_len
    x_next = jnp.concatenate([coefficient[..., 1:, :], coefficient[..., -1:, :]], axis=-2)
    x_prev = jnp.concatenate([coefficient[..., :1, :], coefficient[..., :-1, :]], axis=-2)
    y_next = jnp.concatenate([coefficient[..., edge_len:], coefficient[..., -edge_len:]], axis=-1)
    y_prev = jnp.concatenate([coefficient[..., :edge_len], coefficient[..., :-edge_len]], axis=-1)
    z_next = jnp.where(
        z_index == edge_len - 1,
        coefficient,
        jnp.concatenate([coefficient[..., 1:], coefficient[..., -1:]], axis=-1),
    )
    z_prev = jnp.where(
        z_index == 0,
        coefficient,
        jnp.concatenate([coefficient[..., :1], coefficient[..., :-1]], axis=-1),
    )
    faces = (
        (coefficient + x_next) * 0.5,
        (coefficient + x_prev) * 0.5,
        (coefficient + y_next) * 0.5,
        (coefficient + y_prev) * 0.5,
        (coefficient + z_next) * 0.5,
        (coefficient + z_prev) * 0.5,
    )
    diagonal = REACTION + faces[0]
    for face in faces[1:]:
        diagonal = diagonal + face
    keeps = (
        x_index < edge_len - 1,
        x_index > 0,
        y_index < edge_len - 1,
        y_index > 0,
        z_index < edge_len - 1,
        z_index > 0,
    )
    off_terms = tuple(
        (jnp.where(keep, face, jnp.zeros_like(face)) for keep, face in zip(keeps, faces))
    )
    return (diagonal, off_terms)


def ramp(position, edge_len):
    return jnp.minimum(
        1.0, jnp.minimum((position + 0.5) / MARGIN, (edge_len - position - 0.5) / MARGIN)
    )


def partition(edge_len):
    x_index = lax.broadcasted_iota(jnp.int32, (edge_len, edge_len * edge_len), 0)
    flat_index = lax.broadcasted_iota(jnp.int32, (edge_len, edge_len * edge_len), 1)
    x_float = x_index.astype(jnp.float32)
    y_float = (flat_index // edge_len).astype(jnp.float32)
    return ramp(x_float, edge_len) * ramp(y_float, edge_len)


def blend_weights(edge_len):
    at = np.arange(edge_len, dtype=np.float32)
    lo = (at + np.float32(0.5)) / np.float32(MARGIN)
    hi = (np.float32(edge_len) - at - np.float32(0.5)) / np.float32(MARGIN)
    ramp_np = np.minimum(np.float32(1.0), np.minimum(lo, hi)).astype(np.float32)
    y_of = np.arange(edge_len * edge_len) // edge_len
    return (ramp_np[:, None] * ramp_np[y_of][None, :]).astype(np.float32)


def gram(a, b):
    return lax.dot_general(
        a, b, (((1,), (1,)), ((), ())), precision=HIGHEST, preferred_element_type=jnp.float32
    )


def brick_kernel(
    counts_ref, consts_ref, force_lo, force_hi, coef_ref, blend_ref,
    self_ref, up_ref, lo_ref, col_ref, front_ref, back_ref,
    snap, resid, direc, terms, behind,
    *, edge_len, columns, first,
):
    b = pl.program_id(0)
    last = pl.num_programs(0) - 1
    count = jnp.minimum(counts_ref[first + b], MAX_SWEEPS)
    groups = columns // 8
    plane = edge_len * edge_len
    band = MARGIN * edge_len
    scale_pair = float((MARGIN * edge_len * edge_len) ** (-0.5))

    def rep(row):
        return jnp.concatenate([row] * groups, axis=0)

    coef = coef_ref[...]
    x_at = lax.broadcasted_iota(jnp.int32, (edge_len, plane), 0)
    flat = lax.broadcasted_iota(jnp.int32, (edge_len, plane), 1)
    y_at = flat // edge_len
    z_at = flat % edge_len
    nbrs = (
        jnp.where(x_at == edge_len - 1, coef, pltpu.roll(coef, edge_len - 1, 0)),
        jnp.where(x_at == 0, coef, pltpu.roll(coef, 1, 0)),
        jnp.where(y_at == edge_len - 1, coef, pltpu.roll(coef, plane - edge_len, 1)),
        jnp.where(y_at == 0, coef, pltpu.roll(coef, edge_len, 1)),
        jnp.where(z_at == edge_len - 1, coef, pltpu.roll(coef, plane - 1, 1)),
        jnp.where(z_at == 0, coef, pltpu.roll(coef, 1, 1)),
    )
    faces = [(coef + nb) * 0.5 for nb in nbrs]
    diagonal = REACTION + faces[0]
    for face in faces[1:]:
        diagonal = diagonal + face
    keeps = (
        x_at < edge_len - 1, x_at > 0, y_at < edge_len - 1, y_at > 0, z_at < edge_len - 1, z_at > 0,
    )
    offs = [jnp.where(keep, face, 0.0) for keep, face in zip(keeps, faces)]
    rows_all = [diagonal] + offs + [1.0 / diagonal]
    for k in range(8):
        for x in range(edge_len):
            terms[k, x] = jnp.broadcast_to(rows_all[k][x : x + 1, :], (8, plane))

    def zroll(v, shift):
        return jnp.concatenate(
            [pltpu.roll(v[:, :128], shift, 1), pltpu.roll(v[:, 128:], shift, 1)], axis=1
        )

    start_scale = float(np.float32(1.0 / CENTRE))
    for x in range(edge_len):
        rows = pl.ds(x, columns, stride=edge_len)
        f = jnp.concatenate([force_lo[rows, :], force_hi[rows, :]], axis=1)
        resid[x] = f
        direc[x] = f * rep(terms[7, x]) * start_scale
        snap[x] = jnp.zeros_like(f)

    def sweep(t, carry):
        keep = consts_ref[0, t]
        push = consts_ref[1, t]
        prev = None
        cur = direc[0]
        for x in range(edge_len):
            nxt = direc[x + 1] if x + 1 < edge_len else None
            res = rep(terms[0, x]) * cur
            if nxt is not None:
                res = res - rep(terms[1, x]) * nxt
            if prev is not None:
                res = res - rep(terms[2, x]) * prev
            res = res - rep(terms[3, x]) * pltpu.roll(cur, plane - edge_len, 1)
            res = res - rep(terms[4, x]) * pltpu.roll(cur, edge_len, 1)
            res = res - rep(terms[5, x]) * zroll(cur, 127)
            res = res - rep(terms[6, x]) * zroll(cur, 1)
            r = resid[x] - res
            resid[x] = r
            snap[x] = snap[x] + cur
            direc[x] = keep * cur + rep(push * terms[7, x]) * r
            prev, cur = cur, nxt
        return carry

    lax.fori_loop(0, count, sweep, 0)

    lane = lax.broadcasted_iota(jnp.int32, (columns, plane), 1)
    quarter = [(lane >= band * j) & (lane < band * (j + 1)) for j in range(4)]
    weighted = []
    for x in range(edge_len):
        w = snap[x] * jnp.broadcast_to(blend_ref[x : x + 1, :], (columns, plane))
        weighted.append(w)
    fronts, backs = [], []
    for i in range(edge_len // 4):
        ws = weighted[4 * i : 4 * i + 4]
        f = jnp.where(quarter[0], ws[0], 0.0)
        k = jnp.where(quarter[3], ws[3], 0.0)
        for j in range(1, 4):
            f = jnp.where(quarter[j], pltpu.roll(ws[j], band * j, 1), f)
        for j in range(3):
            k = jnp.where(quarter[j], pltpu.roll(ws[j], band * (j + 1), 1), k)
        fronts.append(f)
        backs.append(k)
    front = jnp.concatenate(fronts, axis=1)
    back = jnp.concatenate(backs, axis=1)
    whole = jnp.concatenate(weighted, axis=1)
    self_ref[...] = gram(whole, whole) / float(edge_len**3)
    up_ref[...] = jnp.concatenate(weighted[:MARGIN], axis=1)
    lo_ref[...] = jnp.concatenate(weighted[edge_len - MARGIN :], axis=1)

    @pl.when(b > 0)
    def _():
        col_ref[b - 1] = gram(behind[...], front) * scale_pair

    behind[...] = back

    @pl.when(b == 0)
    def _():
        front_ref[...] = front

    @pl.when(b == last)
    def _():
        back_ref[...] = back


def run_chunk(force2, coef, blend, consts, counts, first, size):
    bricks, rows2, _ = force2.shape
    edge_len, plane = blend.shape
    columns = rows2 // edge_len
    kernel = functools.partial(brick_kernel, edge_len=edge_len, columns=columns, first=first)
    f32 = jnp.float32
    slab = MARGIN * plane
    band = plane * (edge_len // 4)
    out_shape = (
        jax.ShapeDtypeStruct((size, columns, columns), f32),
        jax.ShapeDtypeStruct((size, columns, slab), f32),
        jax.ShapeDtypeStruct((size, columns, slab), f32),
        jax.ShapeDtypeStruct((size, columns, columns), f32),
        jax.ShapeDtypeStruct((columns, band), f32),
        jax.ShapeDtypeStruct((columns, band), f32),
    )
    grid_spec = pltpu.PrefetchScalarGridSpec(
        num_scalar_prefetch=1,
        grid=(size,),
        in_specs=[
            pl.BlockSpec(memory_space=pltpu.SMEM),
            pl.BlockSpec((None, rows2, 128), lambda b, c: (first + b, 0, 0)),
            pl.BlockSpec((None, rows2, 128), lambda b, c: (first + b, 0, 1)),
            pl.BlockSpec((None, edge_len, plane), lambda b, c: (first + b, 0, 0)),
            pl.BlockSpec((edge_len, plane), lambda b, c: (0, 0)),
        ],
        out_specs=[
            pl.BlockSpec((None, columns, columns), lambda b, c: (b, 0, 0)),
            pl.BlockSpec((None, columns, slab), lambda b, c: (b, 0, 0)),
            pl.BlockSpec((None, columns, slab), lambda b, c: (b, 0, 0)),
            pl.BlockSpec((size, columns, columns), lambda b, c: (0, 0, 0)),
            pl.BlockSpec((columns, band), lambda b, c: (0, 0)),
            pl.BlockSpec((columns, band), lambda b, c: (0, 0)),
        ],
        scratch_shapes=[
            pltpu.VMEM((edge_len, columns, plane), f32),
            pltpu.VMEM((edge_len, columns, plane), f32),
            pltpu.VMEM((edge_len, columns, plane), f32),
            pltpu.VMEM((8, edge_len, 8, plane), f32),
            pltpu.VMEM((columns, band), f32),
        ],
    )
    flops = size * (columns * plane * edge_len * 40 + 2 * columns * columns * plane * edge_len * 6)
    return pl.pallas_call(
        kernel,
        grid_spec=grid_spec,
        out_shape=out_shape,
        compiler_params=pltpu.CompilerParams(dimension_semantics=("arbitrary",)),
        cost_estimate=pl.CostEstimate(
            flops=flops, transcendentals=0, bytes_accessed=size * columns * plane * edge_len * 4
        ),
    )(counts, consts, force2, force2, coef, blend)


CHUNKS = (6, 4, 4, 2)


def on_device(force_columns, coefficient, sweep_counts):
    force = force_columns[0]
    bricks, columns, edge_len, plane = force.shape
    scale_pair = (MARGIN * edge_len * edge_len) ** (-0.5)
    blend = jnp.asarray(blend_weights(edge_len))
    consts = jnp.asarray(np.array(sweep_constants(), np.float32).T)
    force2 = force.reshape(bricks, columns * edge_len, plane)
    counts = sweep_counts[0]
    sizes = CHUNKS if sum(CHUNKS) == bricks else (bricks,)
    firsts = [sum(sizes[:i]) for i in range(len(sizes))]
    selfs, cols, fronts, backs, rows = [], [], [], [], []
    for first, size in zip(firsts, sizes):
        s_c, up_c, lo_c, col_c, front_c, back_c = run_chunk(
            force2, coefficient[0], blend, consts, counts, first, size
        )
        up_in = from_behind(up_c, "wide", -1)
        rows.append(gram3(lo_c, up_in) * scale_pair)
        selfs.append(s_c)
        cols.append(col_c)
        fronts.append(front_c)
        backs.append(back_c)
    fronts.append(from_behind(fronts[0], "narrow", -1))
    joins = gram3(jnp.stack(backs), jnp.stack(fronts[1:])) * scale_pair
    col_parts = []
    for c in range(len(cols)):
        col_parts.append(cols[c][:-1])
        col_parts.append(joins[c][None])
    row_parts = rows
    self_part = jnp.concatenate(selfs, axis=0)
    row_part = jnp.concatenate(row_parts, axis=0)
    col_part = jnp.concatenate(col_parts, axis=0)
    return (
        self_part.reshape(1, bricks, -1),
        row_part.reshape(1, bricks, -1),
        col_part.reshape(1, bricks, -1),
    )


def gram3(a, b):
    return jnp.einsum("bkc,blc->bkl", a, b, precision=HIGHEST)


def solution(mesh):
    in_specs = (
        P("wide", "narrow", None, None, None),
        P("wide", "narrow", None, None),
        P("wide", "narrow"),
    )
    out_specs = (P("wide", "narrow", None), P("wide", "narrow", None), P("wide", "narrow", None))
    return jax.shard_map(
        on_device, mesh=mesh, in_specs=in_specs, out_specs=out_specs, check_vma=False
    )
```

```python
import functools

import numpy as np
import jax
import jax.numpy as jnp
from jax import lax
from jax.experimental import pallas as pl
from jax.experimental.pallas import tpu as pltpu
from jax.sharding import PartitionSpec as P

MARGIN = 4
MAX_SWEEPS = 8

REACTION = 1.0
BOUND_LOW = 0.1
BOUND_HIGH = 2.0
CENTRE = 0.5 * (BOUND_LOW + BOUND_HIGH)
HALF_WIDTH = 0.5 * (BOUND_HIGH - BOUND_LOW)
SIGMA_RATIO = CENTRE / HALF_WIDTH

HIGHEST = lax.Precision.HIGHEST


def sweep_constants():
    rho = np.float32(1.0 / SIGMA_RATIO)
    two_sigma = np.float32(2.0 * SIGMA_RATIO)
    pairs = []
    for _ in range(MAX_SWEEPS):
        rho_next = np.float32(np.float32(1.0) / np.float32(two_sigma - rho))
        keep = np.float32(rho_next * rho)
        push = np.float32(np.float32(np.float32(2.0) * rho_next) / np.float32(HALF_WIDTH))
        pairs.append((float(keep), float(push)))
        rho = rho_next
    return pairs


def from_behind(block, axis, distance):
    devices = range(lax.axis_size(axis))
    route = [((i - distance) % len(devices), i) for i in devices]
    return lax.ppermute(block, axis, route)


def prepare(coefficient):
    edge_len = coefficient.shape[-2]
    plane_len = coefficient.shape[-1]
    x_index = lax.broadcasted_iota(jnp.int32, (edge_len, plane_len), 0)
    flat_index = lax.broadcasted_iota(jnp.int32, (edge_len, plane_len), 1)
    y_index = flat_index // edge_len
    z_index = flat_index % edge_len
    x_next = jnp.concatenate([coefficient[..., 1:, :], coefficient[..., -1:, :]], axis=-2)
    x_prev = jnp.concatenate([coefficient[..., :1, :], coefficient[..., :-1, :]], axis=-2)
    y_next = jnp.concatenate([coefficient[..., edge_len:], coefficient[..., -edge_len:]], axis=-1)
    y_prev = jnp.concatenate([coefficient[..., :edge_len], coefficient[..., :-edge_len]], axis=-1)
    z_next = jnp.where(
        z_index == edge_len - 1,
        coefficient,
        jnp.concatenate([coefficient[..., 1:], coefficient[..., -1:]], axis=-1),
    )
    z_prev = jnp.where(
        z_index == 0,
        coefficient,
        jnp.concatenate([coefficient[..., :1], coefficient[..., :-1]], axis=-1),
    )
    faces = (
        (coefficient + x_next) * 0.5,
        (coefficient + x_prev) * 0.5,
        (coefficient + y_next) * 0.5,
        (coefficient + y_prev) * 0.5,
        (coefficient + z_next) * 0.5,
        (coefficient + z_prev) * 0.5,
    )
    diagonal = REACTION + faces[0]
    for face in faces[1:]:
        diagonal = diagonal + face
    keeps = (
        x_index < edge_len - 1,
        x_index > 0,
        y_index < edge_len - 1,
        y_index > 0,
        z_index < edge_len - 1,
        z_index > 0,
    )
    off_terms = tuple(
        (jnp.where(keep, face, jnp.zeros_like(face)) for keep, face in zip(keeps, faces))
    )
    return (diagonal, off_terms)


def ramp(position, edge_len):
    return jnp.minimum(
        1.0, jnp.minimum((position + 0.5) / MARGIN, (edge_len - position - 0.5) / MARGIN)
    )


def partition(edge_len):
    x_index = lax.broadcasted_iota(jnp.int32, (edge_len, edge_len * edge_len), 0)
    flat_index = lax.broadcasted_iota(jnp.int32, (edge_len, edge_len * edge_len), 1)
    x_float = x_index.astype(jnp.float32)
    y_float = (flat_index // edge_len).astype(jnp.float32)
    return ramp(x_float, edge_len) * ramp(y_float, edge_len)


def blend_weights(edge_len):
    at = np.arange(edge_len, dtype=np.float32)
    lo = (at + np.float32(0.5)) / np.float32(MARGIN)
    hi = (np.float32(edge_len) - at - np.float32(0.5)) / np.float32(MARGIN)
    ramp_np = np.minimum(np.float32(1.0), np.minimum(lo, hi)).astype(np.float32)
    y_of = np.arange(edge_len * edge_len) // edge_len
    return (ramp_np[:, None] * ramp_np[y_of][None, :]).astype(np.float32)


def gram(a, b):
    return lax.dot_general(
        a, b, (((1,), (1,)), ((), ())), precision=HIGHEST, preferred_element_type=jnp.float32
    )


def brick_kernel(
    counts_ref, consts_ref, force_lo, force_hi, coef_ref, blend_ref, behind_in, arrived,
    self_in, col_in, lo_in,
    self_ref, col_ref, lo_ref, up_ref, front_ref, back_ref,
    snap, resid, direc, terms, behind,
    *, edge_len, columns, first, closing,
):
    b = pl.program_id(0)
    last = pl.num_programs(0) - 1
    count = jnp.minimum(counts_ref[first + b], MAX_SWEEPS)
    groups = columns // 8
    plane = edge_len * edge_len
    band = MARGIN * edge_len
    scale_pair = float((MARGIN * edge_len * edge_len) ** (-0.5))

    def rep(row):
        return jnp.concatenate([row] * groups, axis=0)

    coef = coef_ref[...]
    x_at = lax.broadcasted_iota(jnp.int32, (edge_len, plane), 0)
    flat = lax.broadcasted_iota(jnp.int32, (edge_len, plane), 1)
    y_at = flat // edge_len
    z_at = flat % edge_len
    nbrs = (
        jnp.where(x_at == edge_len - 1, coef, pltpu.roll(coef, edge_len - 1, 0)),
        jnp.where(x_at == 0, coef, pltpu.roll(coef, 1, 0)),
        jnp.where(y_at == edge_len - 1, coef, pltpu.roll(coef, plane - edge_len, 1)),
        jnp.where(y_at == 0, coef, pltpu.roll(coef, edge_len, 1)),
        jnp.where(z_at == edge_len - 1, coef, pltpu.roll(coef, plane - 1, 1)),
        jnp.where(z_at == 0, coef, pltpu.roll(coef, 1, 1)),
    )
    faces = [(coef + nb) * 0.5 for nb in nbrs]
    diagonal = REACTION + faces[0]
    for face in faces[1:]:
        diagonal = diagonal + face
    keeps = (
        x_at < edge_len - 1, x_at > 0, y_at < edge_len - 1, y_at > 0, z_at < edge_len - 1, z_at > 0,
    )
    offs = [jnp.where(keep, face, 0.0) for keep, face in zip(keeps, faces)]
    rows_all = [diagonal] + offs + [1.0 / diagonal]
    for k in range(8):
        for x in range(edge_len):
            terms[k, x] = jnp.broadcast_to(rows_all[k][x : x + 1, :], (8, plane))

    def zroll(v, shift):
        return jnp.concatenate(
            [pltpu.roll(v[:, :128], shift, 1), pltpu.roll(v[:, 128:], shift, 1)], axis=1
        )

    start_scale = float(np.float32(1.0 / CENTRE))
    for x in range(edge_len):
        rows = pl.ds(x, columns, stride=edge_len)
        f = jnp.concatenate([force_lo[rows, :], force_hi[rows, :]], axis=1)
        resid[x] = f
        direc[x] = f * rep(terms[7, x]) * start_scale
        snap[x] = jnp.zeros_like(f)

    def sweep(t, carry):
        keep = consts_ref[0, t]
        push = consts_ref[1, t]
        prev = None
        cur = direc[0]
        for x in range(edge_len):
            nxt = direc[x + 1] if x + 1 < edge_len else None
            res = rep(terms[0, x]) * cur
            if nxt is not None:
                res = res - rep(terms[1, x]) * nxt
            if prev is not None:
                res = res - rep(terms[2, x]) * prev
            res = res - rep(terms[3, x]) * pltpu.roll(cur, plane - edge_len, 1)
            res = res - rep(terms[4, x]) * pltpu.roll(cur, edge_len, 1)
            res = res - rep(terms[5, x]) * zroll(cur, 127)
            res = res - rep(terms[6, x]) * zroll(cur, 1)
            r = resid[x] - res
            resid[x] = r
            snap[x] = snap[x] + cur
            direc[x] = keep * cur + rep(push * terms[7, x]) * r
            prev, cur = cur, nxt
        return carry

    lax.fori_loop(0, count, sweep, 0)

    lane = lax.broadcasted_iota(jnp.int32, (columns, plane), 1)
    quarter = [(lane >= band * j) & (lane < band * (j + 1)) for j in range(4)]
    weighted = []
    for x in range(edge_len):
        w = snap[x] * jnp.broadcast_to(blend_ref[x : x + 1, :], (columns, plane))
        weighted.append(w)
    fronts, backs = [], []
    for i in range(edge_len // 4):
        ws = weighted[4 * i : 4 * i + 4]
        f = jnp.where(quarter[0], ws[0], 0.0)
        k = jnp.where(quarter[3], ws[3], 0.0)
        for j in range(1, 4):
            f = jnp.where(quarter[j], pltpu.roll(ws[j], band * j, 1), f)
        for j in range(3):
            k = jnp.where(quarter[j], pltpu.roll(ws[j], band * (j + 1), 1), k)
        fronts.append(f)
        backs.append(k)
    front = jnp.concatenate(fronts, axis=1)
    back = jnp.concatenate(backs, axis=1)
    whole = jnp.concatenate(weighted, axis=1)
    @pl.when(b == 0)
    def _():
        self_ref[...] = self_in[...]
        col_ref[...] = col_in[...]

    self_ref[first + b] = gram(whole, whole) / float(edge_len**3)
    up_ref[...] = jnp.concatenate(weighted[:MARGIN], axis=1)
    lo_ref[...] = jnp.concatenate(weighted[edge_len - MARGIN :], axis=1)

    @pl.when(b == 0)
    def _():
        behind[...] = behind_in[...]

    if first == 0:
        @pl.when(b > 0)
        def _():
            col_ref[b - 1] = gram(behind[...], front) * scale_pair
    else:
        col_ref[first + b - 1] = gram(behind[...], front) * scale_pair
    behind[...] = back
    if closing:
        @pl.when(b == last)
        def _():
            col_ref[first + last] = gram(back, arrived[...]) * scale_pair

    @pl.when(b == 0)
    def _():
        front_ref[...] = front

    @pl.when(b == last)
    def _():
        back_ref[...] = back


def run_chunk(force2, coef, blend, consts, counts, behind_in, arrived, bufs, first, size):
    bricks, rows2, _ = force2.shape
    edge_len, plane = blend.shape
    columns = rows2 // edge_len
    closing = first + size == bricks
    kernel = functools.partial(
        brick_kernel, edge_len=edge_len, columns=columns, first=first, closing=closing
    )
    f32 = jnp.float32
    slab = MARGIN * plane
    band = plane * (edge_len // 4)
    out_shape = (
        jax.ShapeDtypeStruct((bricks, columns, columns), f32),
        jax.ShapeDtypeStruct((bricks, columns, columns), f32),
        jax.ShapeDtypeStruct((bricks, columns, slab), f32),
        jax.ShapeDtypeStruct((size, columns, slab), f32),
        jax.ShapeDtypeStruct((columns, band), f32),
        jax.ShapeDtypeStruct((columns, band), f32),
    )
    whole = lambda b, c: (0, 0, 0)
    grid_spec = pltpu.PrefetchScalarGridSpec(
        num_scalar_prefetch=1,
        grid=(size,),
        in_specs=[
            pl.BlockSpec(memory_space=pltpu.SMEM),
            pl.BlockSpec((None, rows2, 128), lambda b, c: (first + b, 0, 0)),
            pl.BlockSpec((None, rows2, 128), lambda b, c: (first + b, 0, 1)),
            pl.BlockSpec((None, edge_len, plane), lambda b, c: (first + b, 0, 0)),
            pl.BlockSpec((edge_len, plane), lambda b, c: (0, 0)),
            pl.BlockSpec((columns, band), lambda b, c: (0, 0)),
            pl.BlockSpec((columns, band), lambda b, c: (0, 0)),
            pl.BlockSpec((bricks, columns, columns), whole),
            pl.BlockSpec((bricks, columns, columns), whole),
            pl.BlockSpec(memory_space=pl.ANY),
        ],
        out_specs=[
            pl.BlockSpec((bricks, columns, columns), whole),
            pl.BlockSpec((bricks, columns, columns), whole),
            pl.BlockSpec((None, columns, slab), lambda b, c: (first + b, 0, 0)),
            pl.BlockSpec((None, columns, slab), lambda b, c: (b, 0, 0)),
            pl.BlockSpec((columns, band), lambda b, c: (0, 0)),
            pl.BlockSpec((columns, band), lambda b, c: (0, 0)),
        ],
        scratch_shapes=[
            pltpu.VMEM((edge_len, columns, plane), f32),
            pltpu.VMEM((edge_len, columns, plane), f32),
            pltpu.VMEM((edge_len, columns, plane), f32),
            pltpu.VMEM((8, edge_len, 8, plane), f32),
            pltpu.VMEM((columns, band), f32),
        ],
    )
    flops = size * (columns * plane * edge_len * 40 + 2 * columns * columns * plane * edge_len * 6)
    return pl.pallas_call(
        kernel,
        grid_spec=grid_spec,
        out_shape=out_shape,
        compiler_params=pltpu.CompilerParams(dimension_semantics=("arbitrary",)),
        input_output_aliases={8: 0, 9: 1, 10: 2},
        cost_estimate=pl.CostEstimate(
            flops=flops, transcendentals=0, bytes_accessed=size * columns * plane * edge_len * 4
        ),
    )(counts, consts, force2, force2, coef, blend, behind_in, arrived, *bufs)


CHUNKS = (6, 4, 4, 2)


def on_device(force_columns, coefficient, sweep_counts):
    force = force_columns[0]
    bricks, columns, edge_len, plane = force.shape
    scale_pair = (MARGIN * edge_len * edge_len) ** (-0.5)
    blend = jnp.asarray(blend_weights(edge_len))
    consts = jnp.asarray(np.array(sweep_constants(), np.float32).T)
    force2 = force.reshape(bricks, columns * edge_len, plane)
    counts = sweep_counts[0]
    sizes = CHUNKS if sum(CHUNKS) == bricks else (bricks,)
    firsts = [sum(sizes[:i]) for i in range(len(sizes))]
    band = plane * (edge_len // 4)
    behind = jnp.zeros((columns, band), jnp.float32)
    blank = jnp.zeros((columns, band), jnp.float32)
    arrived = blank
    bufs = (
        jnp.zeros((bricks, columns, columns), jnp.float32),
        jnp.zeros((bricks, columns, columns), jnp.float32),
        jnp.zeros((bricks, columns, MARGIN * plane), jnp.float32),
    )
    ups_in = []
    for first, size in zip(firsts, sizes):
        self_b, col_b, lo_b, up_c, front_c, behind = run_chunk(
            force2, coefficient[0], blend, consts, counts, behind,
            arrived if first + size == bricks else blank, bufs, first, size,
        )
        bufs = (self_b, col_b, lo_b)
        if first == 0:
            arrived = from_behind(front_c, "narrow", -1)
        ups_in.append(from_behind(up_c, "wide", -1))
    self_part, col_part, lows = bufs
    row_part = gram3(lows, jnp.concatenate(ups_in, axis=0)) * scale_pair
    return (
        self_part.reshape(1, bricks, -1),
        row_part.reshape(1, bricks, -1),
        col_part.reshape(1, bricks, -1),
    )


def gram3(a, b):
    return jnp.einsum("bkc,blc->bkl", a, b, precision=HIGHEST)


def solution(mesh):
    in_specs = (
        P("wide", "narrow", None, None, None),
        P("wide", "narrow", None, None),
        P("wide", "narrow"),
    )
    out_specs = (P("wide", "narrow", None), P("wide", "narrow", None), P("wide", "narrow", None))
    return jax.shard_map(
        on_device, mesh=mesh, in_specs=in_specs, out_specs=out_specs, check_vma=False
    )
```

```python
import functools

import numpy as np
import jax
import jax.numpy as jnp
from jax import lax
from jax.experimental import pallas as pl
from jax.experimental.pallas import tpu as pltpu
from jax.sharding import PartitionSpec as P

MARGIN = 4
MAX_SWEEPS = 8

REACTION = 1.0
BOUND_LOW = 0.1
BOUND_HIGH = 2.0
CENTRE = 0.5 * (BOUND_LOW + BOUND_HIGH)
HALF_WIDTH = 0.5 * (BOUND_HIGH - BOUND_LOW)
SIGMA_RATIO = CENTRE / HALF_WIDTH

HIGHEST = lax.Precision.HIGHEST


def sweep_constants():
    rho = np.float32(1.0 / SIGMA_RATIO)
    two_sigma = np.float32(2.0 * SIGMA_RATIO)
    pairs = []
    for _ in range(MAX_SWEEPS):
        rho_next = np.float32(np.float32(1.0) / np.float32(two_sigma - rho))
        keep = np.float32(rho_next * rho)
        push = np.float32(np.float32(np.float32(2.0) * rho_next) / np.float32(HALF_WIDTH))
        pairs.append((float(keep), float(push)))
        rho = rho_next
    return pairs


def from_behind(block, axis, distance):
    devices = range(lax.axis_size(axis))
    route = [((i - distance) % len(devices), i) for i in devices]
    return lax.ppermute(block, axis, route)


def prepare(coefficient):
    edge_len = coefficient.shape[-2]
    plane_len = coefficient.shape[-1]
    x_index = lax.broadcasted_iota(jnp.int32, (edge_len, plane_len), 0)
    flat_index = lax.broadcasted_iota(jnp.int32, (edge_len, plane_len), 1)
    y_index = flat_index // edge_len
    z_index = flat_index % edge_len
    x_next = jnp.concatenate([coefficient[..., 1:, :], coefficient[..., -1:, :]], axis=-2)
    x_prev = jnp.concatenate([coefficient[..., :1, :], coefficient[..., :-1, :]], axis=-2)
    y_next = jnp.concatenate([coefficient[..., edge_len:], coefficient[..., -edge_len:]], axis=-1)
    y_prev = jnp.concatenate([coefficient[..., :edge_len], coefficient[..., :-edge_len]], axis=-1)
    z_next = jnp.where(
        z_index == edge_len - 1,
        coefficient,
        jnp.concatenate([coefficient[..., 1:], coefficient[..., -1:]], axis=-1),
    )
    z_prev = jnp.where(
        z_index == 0,
        coefficient,
        jnp.concatenate([coefficient[..., :1], coefficient[..., :-1]], axis=-1),
    )
    faces = (
        (coefficient + x_next) * 0.5,
        (coefficient + x_prev) * 0.5,
        (coefficient + y_next) * 0.5,
        (coefficient + y_prev) * 0.5,
        (coefficient + z_next) * 0.5,
        (coefficient + z_prev) * 0.5,
    )
    diagonal = REACTION + faces[0]
    for face in faces[1:]:
        diagonal = diagonal + face
    keeps = (
        x_index < edge_len - 1,
        x_index > 0,
        y_index < edge_len - 1,
        y_index > 0,
        z_index < edge_len - 1,
        z_index > 0,
    )
    off_terms = tuple(
        (jnp.where(keep, face, jnp.zeros_like(face)) for keep, face in zip(keeps, faces))
    )
    return (diagonal, off_terms)


def ramp(position, edge_len):
    return jnp.minimum(
        1.0, jnp.minimum((position + 0.5) / MARGIN, (edge_len - position - 0.5) / MARGIN)
    )


def partition(edge_len):
    x_index = lax.broadcasted_iota(jnp.int32, (edge_len, edge_len * edge_len), 0)
    flat_index = lax.broadcasted_iota(jnp.int32, (edge_len, edge_len * edge_len), 1)
    x_float = x_index.astype(jnp.float32)
    y_float = (flat_index // edge_len).astype(jnp.float32)
    return ramp(x_float, edge_len) * ramp(y_float, edge_len)


def blend_weights(edge_len):
    at = np.arange(edge_len, dtype=np.float32)
    lo = (at + np.float32(0.5)) / np.float32(MARGIN)
    hi = (np.float32(edge_len) - at - np.float32(0.5)) / np.float32(MARGIN)
    ramp_np = np.minimum(np.float32(1.0), np.minimum(lo, hi)).astype(np.float32)
    y_of = np.arange(edge_len * edge_len) // edge_len
    return (ramp_np[:, None] * ramp_np[y_of][None, :]).astype(np.float32)


def gram(a, b):
    return lax.dot_general(
        a, b, (((1,), (1,)), ((), ())), precision=HIGHEST, preferred_element_type=jnp.float32
    )


def brick_kernel(
    counts_ref, consts_ref, force_lo, force_hi, coef_ref, blend_ref, behind_in, arrived,
    self_in, col_in, lo_in,
    self_ref, col_ref, lo_ref, up_ref, front_ref, back_ref,
    snap, resid, direc, terms, behind,
    *, edge_len, columns, first, closing,
):
    b = pl.program_id(0)
    last = pl.num_programs(0) - 1
    count = jnp.minimum(counts_ref[first + b], MAX_SWEEPS)
    groups = columns // 8
    plane = edge_len * edge_len
    band = MARGIN * edge_len
    scale_pair = float((MARGIN * edge_len * edge_len) ** (-0.5))

    def rep(row):
        return jnp.concatenate([row] * groups, axis=0)

    coef = coef_ref[...]
    x_at = lax.broadcasted_iota(jnp.int32, (edge_len, plane), 0)
    flat = lax.broadcasted_iota(jnp.int32, (edge_len, plane), 1)
    y_at = flat // edge_len
    z_at = flat % edge_len
    nbrs = (
        jnp.where(x_at == edge_len - 1, coef, pltpu.roll(coef, edge_len - 1, 0)),
        jnp.where(x_at == 0, coef, pltpu.roll(coef, 1, 0)),
        jnp.where(y_at == edge_len - 1, coef, pltpu.roll(coef, plane - edge_len, 1)),
        jnp.where(y_at == 0, coef, pltpu.roll(coef, edge_len, 1)),
        jnp.where(z_at == edge_len - 1, coef, pltpu.roll(coef, plane - 1, 1)),
        jnp.where(z_at == 0, coef, pltpu.roll(coef, 1, 1)),
    )
    faces = [(coef + nb) * 0.5 for nb in nbrs]
    diagonal = REACTION + faces[0]
    for face in faces[1:]:
        diagonal = diagonal + face
    keeps = (
        x_at < edge_len - 1, x_at > 0, y_at < edge_len - 1, y_at > 0, z_at < edge_len - 1, z_at > 0,
    )
    offs = [jnp.where(keep, face, 0.0) for keep, face in zip(keeps, faces)]
    rows_all = [diagonal] + offs + [1.0 / diagonal]
    for k in range(8):
        for x in range(edge_len):
            terms[k, x] = jnp.broadcast_to(rows_all[k][x : x + 1, :], (8, plane))

    def zroll(v, shift):
        return jnp.concatenate(
            [pltpu.roll(v[:, :128], shift, 1), pltpu.roll(v[:, 128:], shift, 1)], axis=1
        )

    start_scale = float(np.float32(1.0 / CENTRE))
    for x in range(edge_len):
        rows = pl.ds(x, columns, stride=edge_len)
        f = jnp.concatenate([force_lo[rows, :], force_hi[rows, :]], axis=1)
        resid[x] = f
        direc[x] = f * rep(terms[7, x]) * start_scale
        snap[x] = jnp.zeros_like(f)

    def sweep(t, carry):
        keep = consts_ref[0, t]
        push = consts_ref[1, t]
        prev = None
        cur = direc[0]
        for x in range(edge_len):
            nxt = direc[x + 1] if x + 1 < edge_len else None
            res = rep(terms[0, x]) * cur
            if nxt is not None:
                res = res - rep(terms[1, x]) * nxt
            if prev is not None:
                res = res - rep(terms[2, x]) * prev
            res = res - rep(terms[3, x]) * pltpu.roll(cur, plane - edge_len, 1)
            res = res - rep(terms[4, x]) * pltpu.roll(cur, edge_len, 1)
            res = res - rep(terms[5, x]) * zroll(cur, 127)
            res = res - rep(terms[6, x]) * zroll(cur, 1)
            r = resid[x] - res
            resid[x] = r
            snap[x] = snap[x] + cur
            direc[x] = keep * cur + rep(push * terms[7, x]) * r
            prev, cur = cur, nxt
        return carry

    lax.fori_loop(0, count, sweep, 0)

    lane = lax.broadcasted_iota(jnp.int32, (columns, plane), 1)
    quarter = [(lane >= band * j) & (lane < band * (j + 1)) for j in range(4)]
    weighted = []
    for x in range(edge_len):
        w = snap[x] * jnp.broadcast_to(blend_ref[x : x + 1, :], (columns, plane))
        weighted.append(w)
    fronts, backs = [], []
    for i in range(edge_len // 4):
        ws = weighted[4 * i : 4 * i + 4]
        f = jnp.where(quarter[0], ws[0], 0.0)
        k = jnp.where(quarter[3], ws[3], 0.0)
        for j in range(1, 4):
            f = jnp.where(quarter[j], pltpu.roll(ws[j], band * j, 1), f)
        for j in range(3):
            k = jnp.where(quarter[j], pltpu.roll(ws[j], band * (j + 1), 1), k)
        fronts.append(f)
        backs.append(k)
    front = jnp.concatenate(fronts, axis=1)
    back = jnp.concatenate(backs, axis=1)
    whole = jnp.concatenate(weighted, axis=1)
    if self_in is not None:
        @pl.when(b == 0)
        def _():
            self_ref[...] = self_in[...]
            col_ref[...] = col_in[...]

    self_ref[first + b] = gram(whole, whole) / float(edge_len**3)
    up_ref[...] = jnp.concatenate(weighted[:MARGIN], axis=1)
    lo_ref[...] = jnp.concatenate(weighted[edge_len - MARGIN :], axis=1)

    @pl.when(b == 0)
    def _():
        behind[...] = behind_in[...]

    if first == 0:
        @pl.when(b > 0)
        def _():
            col_ref[b - 1] = gram(behind[...], front) * scale_pair
    else:
        col_ref[first + b - 1] = gram(behind[...], front) * scale_pair
    behind[...] = back
    if closing:
        @pl.when(b == last)
        def _():
            col_ref[first + last] = gram(back, arrived[...]) * scale_pair

    @pl.when(b == 0)
    def _():
        front_ref[...] = front

    @pl.when(b == last)
    def _():
        back_ref[...] = back


def fresh_kernel(*refs, **kw):
    return brick_kernel(*refs[:8], None, None, None, *refs[8:], **kw)


def run_chunk(force2, coef, blend, consts, counts, behind_in, arrived, bufs, first, size):
    bricks, rows2, _ = force2.shape
    edge_len, plane = blend.shape
    columns = rows2 // edge_len
    fresh = bufs is None
    kernel = functools.partial(
        fresh_kernel if fresh else brick_kernel,
        edge_len=edge_len, columns=columns, first=first, closing=False,
    )
    f32 = jnp.float32
    slab = MARGIN * plane
    band = plane * (edge_len // 4)
    out_shape = (
        jax.ShapeDtypeStruct((bricks, columns, columns), f32),
        jax.ShapeDtypeStruct((bricks, columns, columns), f32),
        jax.ShapeDtypeStruct((bricks, columns, slab), f32),
        jax.ShapeDtypeStruct((size, columns, slab), f32),
        jax.ShapeDtypeStruct((columns, band), f32),
        jax.ShapeDtypeStruct((columns, band), f32),
    )
    whole = lambda b, c: (0, 0, 0)
    grid_spec = pltpu.PrefetchScalarGridSpec(
        num_scalar_prefetch=1,
        grid=(size,),
        in_specs=[
            pl.BlockSpec(memory_space=pltpu.SMEM),
            pl.BlockSpec((None, rows2, 128), lambda b, c: (first + b, 0, 0)),
            pl.BlockSpec((None, rows2, 128), lambda b, c: (first + b, 0, 1)),
            pl.BlockSpec((None, edge_len, plane), lambda b, c: (first + b, 0, 0)),
            pl.BlockSpec((edge_len, plane), lambda b, c: (0, 0)),
            pl.BlockSpec((columns, band), lambda b, c: (0, 0)),
            pl.BlockSpec((columns, band), lambda b, c: (0, 0)),
        ] + ([] if fresh else [
            pl.BlockSpec((bricks, columns, columns), whole),
            pl.BlockSpec((bricks, columns, columns), whole),
            pl.BlockSpec(memory_space=pl.ANY),
        ]),
        out_specs=[
            pl.BlockSpec((bricks, columns, columns), whole),
            pl.BlockSpec((bricks, columns, columns), whole),
            pl.BlockSpec((None, columns, slab), lambda b, c: (first + b, 0, 0)),
            pl.BlockSpec((None, columns, slab), lambda b, c: (b, 0, 0)),
            pl.BlockSpec((columns, band), lambda b, c: (0, 0)),
            pl.BlockSpec((columns, band), lambda b, c: (0, 0)),
        ],
        scratch_shapes=[
            pltpu.VMEM((edge_len, columns, plane), f32),
            pltpu.VMEM((edge_len, columns, plane), f32),
            pltpu.VMEM((edge_len, columns, plane), f32),
            pltpu.VMEM((8, edge_len, 8, plane), f32),
            pltpu.VMEM((columns, band), f32),
        ],
    )
    flops = size * (columns * plane * edge_len * 40 + 2 * columns * columns * plane * edge_len * 6)
    return pl.pallas_call(
        kernel,
        grid_spec=grid_spec,
        out_shape=out_shape,
        compiler_params=pltpu.CompilerParams(dimension_semantics=("arbitrary",)),
        input_output_aliases={} if fresh else {8: 0, 9: 1, 10: 2},
        cost_estimate=pl.CostEstimate(
            flops=flops, transcendentals=0, bytes_accessed=size * columns * plane * edge_len * 4
        ),
    )(counts, consts, force2, force2, coef, blend, behind_in, arrived, *(bufs or ()))


CHUNKS = (6, 4, 4, 2)


def on_device(force_columns, coefficient, sweep_counts):
    force = force_columns[0]
    bricks, columns, edge_len, plane = force.shape
    scale_pair = (MARGIN * edge_len * edge_len) ** (-0.5)
    blend = jnp.asarray(blend_weights(edge_len))
    consts = jnp.asarray(np.array(sweep_constants(), np.float32).T)
    force2 = force.reshape(bricks, columns * edge_len, plane)
    counts = sweep_counts[0]
    sizes = CHUNKS if sum(CHUNKS) == bricks else (bricks,)
    firsts = [sum(sizes[:i]) for i in range(len(sizes))]
    band = plane * (edge_len // 4)
    blank = jnp.zeros((columns, band), jnp.float32)
    behind = blank
    bufs = None
    ups_in = []
    for first, size in zip(firsts, sizes):
        self_b, col_b, lo_b, up_c, front_c, behind = run_chunk(
            force2, coefficient[0], blend, consts, counts, behind, blank, bufs, first, size
        )
        bufs = (self_b, col_b, lo_b)
        if first == 0:
            arrived = from_behind(front_c, "narrow", -1)
        ups_in.append(from_behind(up_c, "wide", -1))
    self_part, col_part, lows = bufs
    closing_col = gram(behind, arrived) * scale_pair
    col_part = col_part.at[bricks - 1].set(closing_col)
    row_part = gram3(lows, jnp.concatenate(ups_in, axis=0)) * scale_pair
    return (
        self_part.reshape(1, bricks, -1),
        row_part.reshape(1, bricks, -1),
        col_part.reshape(1, bricks, -1),
    )


def gram3(a, b):
    return jnp.einsum("bkc,blc->bkl", a, b, precision=HIGHEST)


def solution(mesh):
    in_specs = (
        P("wide", "narrow", None, None, None),
        P("wide", "narrow", None, None),
        P("wide", "narrow"),
    )
    out_specs = (P("wide", "narrow", None), P("wide", "narrow", None), P("wide", "narrow", None))
    return jax.shard_map(
        on_device, mesh=mesh, in_specs=in_specs, out_specs=out_specs, check_vma=False
    )
```

```python
import functools

import numpy as np
import jax
import jax.numpy as jnp
from jax import lax
from jax.experimental import pallas as pl
from jax.experimental.pallas import tpu as pltpu
from jax.sharding import PartitionSpec as P

MARGIN = 4
MAX_SWEEPS = 8

REACTION = 1.0
BOUND_LOW = 0.1
BOUND_HIGH = 2.0
CENTRE = 0.5 * (BOUND_LOW + BOUND_HIGH)
HALF_WIDTH = 0.5 * (BOUND_HIGH - BOUND_LOW)
SIGMA_RATIO = CENTRE / HALF_WIDTH

HIGHEST = lax.Precision.HIGH


def sweep_constants():
    rho = np.float32(1.0 / SIGMA_RATIO)
    two_sigma = np.float32(2.0 * SIGMA_RATIO)
    pairs = []
    for _ in range(MAX_SWEEPS):
        rho_next = np.float32(np.float32(1.0) / np.float32(two_sigma - rho))
        keep = np.float32(rho_next * rho)
        push = np.float32(np.float32(np.float32(2.0) * rho_next) / np.float32(HALF_WIDTH))
        pairs.append((float(keep), float(push)))
        rho = rho_next
    return pairs


def from_behind(block, axis, distance):
    devices = range(lax.axis_size(axis))
    route = [((i - distance) % len(devices), i) for i in devices]
    return lax.ppermute(block, axis, route)


def prepare(coefficient):
    edge_len = coefficient.shape[-2]
    plane_len = coefficient.shape[-1]
    x_index = lax.broadcasted_iota(jnp.int32, (edge_len, plane_len), 0)
    flat_index = lax.broadcasted_iota(jnp.int32, (edge_len, plane_len), 1)
    y_index = flat_index // edge_len
    z_index = flat_index % edge_len
    x_next = jnp.concatenate([coefficient[..., 1:, :], coefficient[..., -1:, :]], axis=-2)
    x_prev = jnp.concatenate([coefficient[..., :1, :], coefficient[..., :-1, :]], axis=-2)
    y_next = jnp.concatenate([coefficient[..., edge_len:], coefficient[..., -edge_len:]], axis=-1)
    y_prev = jnp.concatenate([coefficient[..., :edge_len], coefficient[..., :-edge_len]], axis=-1)
    z_next = jnp.where(
        z_index == edge_len - 1,
        coefficient,
        jnp.concatenate([coefficient[..., 1:], coefficient[..., -1:]], axis=-1),
    )
    z_prev = jnp.where(
        z_index == 0,
        coefficient,
        jnp.concatenate([coefficient[..., :1], coefficient[..., :-1]], axis=-1),
    )
    faces = (
        (coefficient + x_next) * 0.5,
        (coefficient + x_prev) * 0.5,
        (coefficient + y_next) * 0.5,
        (coefficient + y_prev) * 0.5,
        (coefficient + z_next) * 0.5,
        (coefficient + z_prev) * 0.5,
    )
    diagonal = REACTION + faces[0]
    for face in faces[1:]:
        diagonal = diagonal + face
    keeps = (
        x_index < edge_len - 1,
        x_index > 0,
        y_index < edge_len - 1,
        y_index > 0,
        z_index < edge_len - 1,
        z_index > 0,
    )
    off_terms = tuple(
        (jnp.where(keep, face, jnp.zeros_like(face)) for keep, face in zip(keeps, faces))
    )
    return (diagonal, off_terms)


def ramp(position, edge_len):
    return jnp.minimum(
        1.0, jnp.minimum((position + 0.5) / MARGIN, (edge_len - position - 0.5) / MARGIN)
    )


def partition(edge_len):
    x_index = lax.broadcasted_iota(jnp.int32, (edge_len, edge_len * edge_len), 0)
    flat_index = lax.broadcasted_iota(jnp.int32, (edge_len, edge_len * edge_len), 1)
    x_float = x_index.astype(jnp.float32)
    y_float = (flat_index // edge_len).astype(jnp.float32)
    return ramp(x_float, edge_len) * ramp(y_float, edge_len)


def blend_weights(edge_len):
    at = np.arange(edge_len, dtype=np.float32)
    lo = (at + np.float32(0.5)) / np.float32(MARGIN)
    hi = (np.float32(edge_len) - at - np.float32(0.5)) / np.float32(MARGIN)
    ramp_np = np.minimum(np.float32(1.0), np.minimum(lo, hi)).astype(np.float32)
    y_of = np.arange(edge_len * edge_len) // edge_len
    return (ramp_np[:, None] * ramp_np[y_of][None, :]).astype(np.float32)


def gram(a, b):
    return lax.dot_general(
        a, b, (((1,), (1,)), ((), ())), precision=HIGHEST, preferred_element_type=jnp.float32
    )


def brick_kernel(
    counts_ref, consts_ref, force_lo, force_hi, coef_ref, blend_ref, behind_in, arrived,
    self_in, col_in, lo_in,
    self_ref, col_ref, lo_ref, up_ref, front_ref, back_ref,
    snap, resid, direc, terms, behind,
    *, edge_len, columns, first, closing,
):
    b = pl.program_id(0)
    last = pl.num_programs(0) - 1
    count = jnp.minimum(counts_ref[first + b], MAX_SWEEPS)
    groups = columns // 8
    plane = edge_len * edge_len
    band = MARGIN * edge_len
    scale_pair = float((MARGIN * edge_len * edge_len) ** (-0.5))

    def rep(row):
        return jnp.concatenate([row] * groups, axis=0)

    coef = coef_ref[...]
    x_at = lax.broadcasted_iota(jnp.int32, (edge_len, plane), 0)
    flat = lax.broadcasted_iota(jnp.int32, (edge_len, plane), 1)
    y_at = flat // edge_len
    z_at = flat % edge_len
    nbrs = (
        jnp.where(x_at == edge_len - 1, coef, pltpu.roll(coef, edge_len - 1, 0)),
        jnp.where(x_at == 0, coef, pltpu.roll(coef, 1, 0)),
        jnp.where(y_at == edge_len - 1, coef, pltpu.roll(coef, plane - edge_len, 1)),
        jnp.where(y_at == 0, coef, pltpu.roll(coef, edge_len, 1)),
        jnp.where(z_at == edge_len - 1, coef, pltpu.roll(coef, plane - 1, 1)),
        jnp.where(z_at == 0, coef, pltpu.roll(coef, 1, 1)),
    )
    faces = [(coef + nb) * 0.5 for nb in nbrs]
    diagonal = REACTION + faces[0]
    for face in faces[1:]:
        diagonal = diagonal + face
    keeps = (
        x_at < edge_len - 1, x_at > 0, y_at < edge_len - 1, y_at > 0, z_at < edge_len - 1, z_at > 0,
    )
    offs = [jnp.where(keep, face, 0.0) for keep, face in zip(keeps, faces)]
    rows_all = [diagonal] + offs + [1.0 / diagonal]
    for k in range(8):
        for x in range(edge_len):
            terms[k, x] = jnp.broadcast_to(rows_all[k][x : x + 1, :], (8, plane))

    def zroll(v, shift):
        return jnp.concatenate(
            [pltpu.roll(v[:, :128], shift, 1), pltpu.roll(v[:, 128:], shift, 1)], axis=1
        )

    start_scale = float(np.float32(1.0 / CENTRE))
    for x in range(edge_len):
        rows = pl.ds(x, columns, stride=edge_len)
        f = jnp.concatenate([force_lo[rows, :], force_hi[rows, :]], axis=1)
        resid[x] = f
        direc[x] = f * rep(terms[7, x]) * start_scale
        snap[x] = jnp.zeros_like(f)

    def sweep(t, carry):
        keep = consts_ref[0, t]
        push = consts_ref[1, t]
        prev = None
        cur = direc[0]
        for x in range(edge_len):
            nxt = direc[x + 1] if x + 1 < edge_len else None
            res = rep(terms[0, x]) * cur
            if nxt is not None:
                res = res - rep(terms[1, x]) * nxt
            if prev is not None:
                res = res - rep(terms[2, x]) * prev
            res = res - rep(terms[3, x]) * pltpu.roll(cur, plane - edge_len, 1)
            res = res - rep(terms[4, x]) * pltpu.roll(cur, edge_len, 1)
            res = res - rep(terms[5, x]) * zroll(cur, 127)
            res = res - rep(terms[6, x]) * zroll(cur, 1)
            r = resid[x] - res
            resid[x] = r
            snap[x] = snap[x] + cur
            direc[x] = keep * cur + rep(push * terms[7, x]) * r
            prev, cur = cur, nxt
        return carry

    lax.fori_loop(0, count, sweep, 0)

    lane = lax.broadcasted_iota(jnp.int32, (columns, plane), 1)
    quarter = [(lane >= band * j) & (lane < band * (j + 1)) for j in range(4)]
    weighted = []
    for x in range(edge_len):
        w = snap[x] * jnp.broadcast_to(blend_ref[x : x + 1, :], (columns, plane))
        weighted.append(w)
    fronts, backs = [], []
    for i in range(edge_len // 4):
        ws = weighted[4 * i : 4 * i + 4]
        f = jnp.where(quarter[0], ws[0], 0.0)
        k = jnp.where(quarter[3], ws[3], 0.0)
        for j in range(1, 4):
            f = jnp.where(quarter[j], pltpu.roll(ws[j], band * j, 1), f)
        for j in range(3):
            k = jnp.where(quarter[j], pltpu.roll(ws[j], band * (j + 1), 1), k)
        fronts.append(f)
        backs.append(k)
    front = jnp.concatenate(fronts, axis=1)
    back = jnp.concatenate(backs, axis=1)
    whole = jnp.concatenate(weighted, axis=1)
    if self_in is not None:
        @pl.when(b == 0)
        def _():
            self_ref[...] = self_in[...]
            col_ref[...] = col_in[...]

    self_ref[first + b] = gram(whole, whole) / float(edge_len**3)
    up_ref[...] = jnp.concatenate(weighted[:MARGIN], axis=1)
    lo_ref[...] = jnp.concatenate(weighted[edge_len - MARGIN :], axis=1)

    @pl.when(b == 0)
    def _():
        behind[...] = behind_in[...]

    if first == 0:
        @pl.when(b > 0)
        def _():
            col_ref[b - 1] = gram(behind[...], front) * scale_pair
    else:
        col_ref[first + b - 1] = gram(behind[...], front) * scale_pair
    behind[...] = back
    if closing:
        @pl.when(b == last)
        def _():
            col_ref[first + last] = gram(back, arrived[...]) * scale_pair

    @pl.when(b == 0)
    def _():
        front_ref[...] = front

    @pl.when(b == last)
    def _():
        back_ref[...] = back


def fresh_kernel(*refs, **kw):
    return brick_kernel(*refs[:8], None, None, None, *refs[8:], **kw)


def run_chunk(force2, coef, blend, consts, counts, behind_in, arrived, bufs, first, size):
    bricks, rows2, _ = force2.shape
    edge_len, plane = blend.shape
    columns = rows2 // edge_len
    fresh = bufs is None
    kernel = functools.partial(
        fresh_kernel if fresh else brick_kernel,
        edge_len=edge_len, columns=columns, first=first, closing=False,
    )
    f32 = jnp.float32
    slab = MARGIN * plane
    band = plane * (edge_len // 4)
    out_shape = (
        jax.ShapeDtypeStruct((bricks, columns, columns), f32),
        jax.ShapeDtypeStruct((bricks, columns, columns), f32),
        jax.ShapeDtypeStruct((bricks, columns, slab), f32),
        jax.ShapeDtypeStruct((size, columns, slab), f32),
        jax.ShapeDtypeStruct((columns, band), f32),
        jax.ShapeDtypeStruct((columns, band), f32),
    )
    whole = lambda b, c: (0, 0, 0)
    grid_spec = pltpu.PrefetchScalarGridSpec(
        num_scalar_prefetch=1,
        grid=(size,),
        in_specs=[
            pl.BlockSpec(memory_space=pltpu.SMEM),
            pl.BlockSpec((None, rows2, 128), lambda b, c: (first + b, 0, 0)),
            pl.BlockSpec((None, rows2, 128), lambda b, c: (first + b, 0, 1)),
            pl.BlockSpec((None, edge_len, plane), lambda b, c: (first + b, 0, 0)),
            pl.BlockSpec((edge_len, plane), lambda b, c: (0, 0)),
            pl.BlockSpec((columns, band), lambda b, c: (0, 0)),
            pl.BlockSpec((columns, band), lambda b, c: (0, 0)),
        ] + ([] if fresh else [
            pl.BlockSpec((bricks, columns, columns), whole),
            pl.BlockSpec((bricks, columns, columns), whole),
            pl.BlockSpec(memory_space=pl.ANY),
        ]),
        out_specs=[
            pl.BlockSpec((bricks, columns, columns), whole),
            pl.BlockSpec((bricks, columns, columns), whole),
            pl.BlockSpec((None, columns, slab), lambda b, c: (first + b, 0, 0)),
            pl.BlockSpec((None, columns, slab), lambda b, c: (b, 0, 0)),
            pl.BlockSpec((columns, band), lambda b, c: (0, 0)),
            pl.BlockSpec((columns, band), lambda b, c: (0, 0)),
        ],
        scratch_shapes=[
            pltpu.VMEM((edge_len, columns, plane), f32),
            pltpu.VMEM((edge_len, columns, plane), f32),
            pltpu.VMEM((edge_len, columns, plane), f32),
            pltpu.VMEM((8, edge_len, 8, plane), f32),
            pltpu.VMEM((columns, band), f32),
        ],
    )
    flops = size * (columns * plane * edge_len * 40 + 2 * columns * columns * plane * edge_len * 6)
    return pl.pallas_call(
        kernel,
        grid_spec=grid_spec,
        out_shape=out_shape,
        compiler_params=pltpu.CompilerParams(dimension_semantics=("arbitrary",)),
        input_output_aliases={} if fresh else {8: 0, 9: 1, 10: 2},
        cost_estimate=pl.CostEstimate(
            flops=flops, transcendentals=0, bytes_accessed=size * columns * plane * edge_len * 4
        ),
    )(counts, consts, force2, force2, coef, blend, behind_in, arrived, *(bufs or ()))


CHUNKS = (6, 4, 4, 2)


def on_device(force_columns, coefficient, sweep_counts):
    force = force_columns[0]
    bricks, columns, edge_len, plane = force.shape
    scale_pair = (MARGIN * edge_len * edge_len) ** (-0.5)
    blend = jnp.asarray(blend_weights(edge_len))
    consts = jnp.asarray(np.array(sweep_constants(), np.float32).T)
    force2 = force.reshape(bricks, columns * edge_len, plane)
    counts = sweep_counts[0]
    sizes = CHUNKS if sum(CHUNKS) == bricks else (bricks,)
    firsts = [sum(sizes[:i]) for i in range(len(sizes))]
    band = plane * (edge_len // 4)
    blank = jnp.zeros((columns, band), jnp.float32)
    behind = blank
    bufs = None
    ups_in = []
    for first, size in zip(firsts, sizes):
        self_b, col_b, lo_b, up_c, front_c, behind = run_chunk(
            force2, coefficient[0], blend, consts, counts, behind, blank, bufs, first, size
        )
        bufs = (self_b, col_b, lo_b)
        if first == 0:
            arrived = from_behind(front_c, "narrow", -1)
        ups_in.append(from_behind(up_c, "wide", -1))
    self_part, col_part, lows = bufs
    closing_col = gram(behind, arrived) * scale_pair
    col_part = col_part.at[bricks - 1].set(closing_col)
    row_part = gram3(lows, jnp.concatenate(ups_in, axis=0)) * scale_pair
    return (
        self_part.reshape(1, bricks, -1),
        row_part.reshape(1, bricks, -1),
        col_part.reshape(1, bricks, -1),
    )


def gram3(a, b):
    return jnp.einsum("bkc,blc->bkl", a, b, precision=HIGHEST)


def solution(mesh):
    in_specs = (
        P("wide", "narrow", None, None, None),
        P("wide", "narrow", None, None),
        P("wide", "narrow"),
    )
    out_specs = (P("wide", "narrow", None), P("wide", "narrow", None), P("wide", "narrow", None))
    return jax.shard_map(
        on_device, mesh=mesh, in_specs=in_specs, out_specs=out_specs, check_vma=False
    )
```
